512 devices in a mesh: blk: 64 (over x, z), head: 8 (over y, core).
Axes of the slice: x: 4, y: 4, z: 16, core: 2. Of those that a mesh axis runs over, the one named last changes fastest.
Arguments:
- acceptance_vector: bfloat16 [8192, 4096], P('blk', 'head'), may hold values from -6 to 6
- lookup_vector_array: bfloat16 [8192, 4096], P('blk', 'head'), may hold values from -2 to 2
- payload_vector_array: bfloat16 [8192, 4096], P('blk', 'head'), may hold values from -6 to 6
- raw_gating_signal: bfloat16 [8192, 4096], P('blk', 'head'), may hold values from -6 to 6
- raw_forgetting_rate: bfloat16 [8192, 4096], P('blk', 'head'), may hold values from -16 to 1
- current_reward_vector: float32 [4096], P('head'), may hold values from -1.5 to 1.5
- memory_following_query: bfloat16 [2, 4096, 64], P(None, 'head'), may hold values from -24 to 24
- group_layernorm_scaling: float32 [4096], P('head'), may hold values from 0.25 to 1.75
- closing_layernorm_scaling: float32 [4096], replicated, may hold values from 0.25 to 1.75
- skip_stream_input: bfloat16 [8192, 4096], P(('blk', 'head')), may hold values from -6 to 6
- closing_projection: bfloat16 [4096, 4096], P('head', 'blk'), may hold values from -0.09375 to 0.09375
- vocabulary_readout: bfloat16 [32768, 4096], P('blk'), may hold values from -15.625 to 15.625
- following_labels: int32 [8192], P(('blk', 'head')), may hold values from 0 to 32767
- response_indicator: int32 [8192], P(('blk', 'head')), may hold values 0 or 1
- baseline_logarithmic_likelihood: float32 [8192], P(('blk', 'head')), may hold values from -14 to -6
- rollout_for_segment: int32 [64], replicated, may hold values from 0 to 15, never falling along the last dimension, each value on 1 to 32 neighbouring positions
- query_text_for_rollout: int32 [16], replicated, may hold values from 0 to 1
Outputs:
- token_ratio: float32 [8192], P(('blk', 'head'))
- seq_ratio: float32 [16], replicated
The draws below stay inside these ranges and needn't reach their ends.
Inputs may be any that keep to these rules, and one draw needn't show every extreme that they name: `rollout_for_segment`: sequences fill whole consecutive blocks, each 1 to 32 blocks, one exactly 32; ids start at 0 and rise by one at each new sequence.
All inputs are finite; a program needn't handle non-finite values. No bound on the sum of `response_indicator` on one device may be relied on, other than what follows from the above.
Results may differ from the reference program's by a relative error of at most 0.0017.
Values may be sent and summed in bfloat16 or wider, within the bound.
No kernel may reach another device: no remote copies, remote signals or barrier semaphores. Data moves between devices by JAX's collectives and lax.ppermute only.
A program may use at most 128 MiB of HBM per device.

```python
import math
import jax
import jax.numpy as jnp
import numpy as np
from jax import lax

ATTENTION_GROUPS = 64
GROUP_DIMENSION = 64
EMBED_DIMENSION = 4096
VOCAB = 32768
TOK_BLK = 128
MOST_BLK = 32
PROMPTS = 2
BLOCKS = 64
SEQS = 16
TOKEN_TOTAL = 8192


def draw_raw_forgetting_rate(key, part):
    lookup_vectors = jax.random.split(key, 7)
    linked_series = TOK_BLK * MOST_BLK
    fast = jax.random.randint(lookup_vectors[0], (ATTENTION_GROUPS,), 0, 2) == 0
    slow_rate = jnp.exp(jax.random.uniform(lookup_vectors[1], (ATTENTION_GROUPS,), jnp.float32, jnp.log(0.05), jnp.log(0.5))) / linked_series
    fast_rate = jnp.exp(jax.random.uniform(lookup_vectors[2], (ATTENTION_GROUPS,), jnp.float32, jnp.log(1.0 / 50.0), jnp.log(1.0 / 30.0)))
    speed_factor = jnp.repeat(jnp.where(fast, fast_rate, slow_rate), GROUP_DIMENSION)
    small_noise = jnp.exp(jax.random.uniform(lookup_vectors[3], (TOKEN_TOTAL, EMBED_DIMENSION), jnp.float32, -0.7, 0.7))
    block_share = jnp.exp(jax.random.uniform(lookup_vectors[4], (TOKEN_TOTAL // TOK_BLK, 1), jnp.float32, -0.7, 0.7))
    block_share = jnp.repeat(block_share, TOK_BLK, axis=0)
    sudden_spike = (jax.random.randint(lookup_vectors[5], (TOKEN_TOTAL, 1), 0, linked_series) < 4).astype(jnp.float32)
    dropped_amount = jax.random.uniform(lookup_vectors[6], (TOKEN_TOTAL, 1), jnp.float32, 0.2, 0.5)
    grand_sum = speed_factor[None, :] * small_noise * block_share + sudden_spike * -jnp.log(1.0 - dropped_amount)
    return jnp.log(grand_sum).astype(jnp.bfloat16)


def draw_vocabulary_readout(key, part):
    lookup_vectors = jax.random.split(key, 1)
    base = jnp.clip(jax.random.normal(lookup_vectors[0], (VOCAB, EMBED_DIMENSION), jnp.float32), -6.0, 6.0) * 3.0 * EMBED_DIMENSION ** (-0.5)
    return base.astype(jnp.bfloat16)


def set_ends(entries, stream_key, low, top_value):
    index_at = [jax.random.randint(jax.random.fold_in(stream_key, axis), (), 0, length) for axis, length in enumerate(entries.shape)]
    main_axis = entries.shape.index(max(entries.shape))
    neighbour = index_at[:main_axis] + [(index_at[main_axis] + 1) % entries.shape[main_axis]] + index_at[main_axis + 1:]
    return entries.at[tuple(index_at)].set(low).at[tuple(neighbour)].set(top_value)


def levels(own_key, shape, shards, smallest, high):
    factor_of = 1.0
    for dim, shards_of in shards:
        draws = jax.random.uniform(jax.random.fold_in(jax.random.fold_in(own_key, 6), dim), (shards_of,), jnp.float32, smallest / len(shards), high / len(shards))
        factor_of = factor_of * jnp.repeat(jnp.exp(draws), shape[dim] // shards_of).reshape((-1,) + (1,) * (len(shape) - 1 - dim))
    return factor_of


def rank_table(number_of, slope):
    weights = [(1 << 20) // math.isqrt(standing ** slope) + 1 for standing in range(1, number_of + 1)]
    scale = 1 + sum(weights) // (1 << 30)
    return np.cumsum(np.array([max(1, weight // scale) for weight in weights]))


def ranked(own_key, shape, count, slope):
    table = rank_table(count, slope)
    ticket = jax.random.randint(jax.random.fold_in(own_key, 1), shape, 0, int(table[count - 1]))
    standing = jnp.searchsorted(jnp.asarray(table, jnp.int32), ticket, side="right")
    return jax.random.permutation(jax.random.fold_in(own_key, 2), count)[standing].astype(jnp.int32)


def length_profile(count, total, most, skew):
    weights = [(1 << 20) // math.isqrt(grade ** skew) + 1 for grade in range(2, count + 1)]
    rest, counts = total - most - (count - 1), [1] * (count - 1)
    while rest > 0:
        free = [i for i in range(count - 1) if counts[i] < most]
        whole, remaining = sum([weights[i] for i in free]), rest
        for i in free:
            extra = min(most - counts[i], max(1, remaining * weights[i] // whole), rest)
            counts[i] = counts[i] + extra
            rest = rest - extra
    return np.array([most] + counts)


def uneven(stream_key, count, total, reach, lean):
    if count == 2:
        one = jax.random.randint(stream_key, (), max(1, total - reach), min(reach, total - 1) + 1)
        return jnp.stack([one, total - one])
    sizes = jnp.asarray(length_profile(count, total, reach, lean), jnp.int32)
    pairs = (count - 1) // 2
    giver, receiver = sizes[1:1 + 2 * pairs:2], sizes[2:2 + 2 * pairs:2]
    margin = jnp.minimum(giver - 1, reach - receiver)
    moved = jax.random.randint(jax.random.fold_in(stream_key, 1), (pairs,), 0, 1 << 20) % (margin + 1)
    sizes = sizes.at[1:1 + 2 * pairs:2].set(giver - moved).at[2:2 + 2 * pairs:2].set(receiver + moved)
    return sizes[jax.random.permutation(jax.random.fold_in(stream_key, 2), count)]


def normal_values(rng, extent, deviation, most, shards=(), kind=jnp.bfloat16):
    result = deviation * jax.random.normal(rng, extent, jnp.float32)
    if shards:
        result = result * levels(rng, extent, shards, -0.22, 0.18)
    return jnp.clip(result, -most, most).astype(kind)


def setup_inputs(seed: int = 0) -> dict:
    keys = jax.random.split(jax.random.key(seed), 18)
    return {
        "acceptance_vector": normal_values(keys[0], (TOKEN_TOTAL, EMBED_DIMENSION), 1.0, 6.0, ((0, 64), (1, 8))),
        "lookup_vector_array": normal_values(keys[1], (TOKEN_TOTAL, EMBED_DIMENSION), 0.3, 2.0, ((0, 64), (1, 8))),
        "payload_vector_array": normal_values(keys[2], (TOKEN_TOTAL, EMBED_DIMENSION), 1.0, 6.0, ((0, 64), (1, 8))),
        "raw_gating_signal": normal_values(keys[3], (TOKEN_TOTAL, EMBED_DIMENSION), 1.5, 6.0, ((0, 64), (1, 8))),
        "raw_forgetting_rate": draw_raw_forgetting_rate(jax.random.fold_in(keys[17], 71), 0),
        "current_reward_vector": jnp.clip(jax.random.uniform(keys[5], (EMBED_DIMENSION,), jnp.float32, -1.5, 1.5) * levels(keys[5], (EMBED_DIMENSION,), ((0, 8),), -0.4, 0.0), -1.5, 1.5),
        "memory_following_query": normal_values(keys[6], (PROMPTS, EMBED_DIMENSION, GROUP_DIMENSION), 4.0, 24.0, ((1, 8),)),
        "group_layernorm_scaling": jnp.clip(1.0 + 0.15 * jax.random.normal(keys[7], (EMBED_DIMENSION,), jnp.float32), 0.25, 1.75),
        "closing_layernorm_scaling": jnp.clip(1.0 + 0.15 * jax.random.normal(keys[8], (EMBED_DIMENSION,), jnp.float32), 0.25, 1.75),
        "skip_stream_input": normal_values(keys[9], (TOKEN_TOTAL, EMBED_DIMENSION), 1.0, 6.0, ((0, 512),)),
        "closing_projection": normal_values(keys[10], (EMBED_DIMENSION, EMBED_DIMENSION), EMBED_DIMENSION ** -0.5, 0.09375, ((0, 8), (1, 64))),
        "vocabulary_readout": draw_vocabulary_readout(jax.random.fold_in(keys[17], 71), 0),
        "following_labels": set_ends(ranked(keys[12], (TOKEN_TOTAL,), VOCAB, 2), jax.random.fold_in(keys[12], 3), 0, VOCAB - 1).astype(jnp.int32),
        "response_indicator": set_ends((jax.random.randint(keys[13], (TOKEN_TOTAL,), 0, 2) < 1).astype(jnp.int32), jax.random.fold_in(keys[13], 1), 0, 1),
        "baseline_logarithmic_likelihood": jnp.clip(-14.0 + 8.0 * jax.random.uniform(keys[14], (TOKEN_TOTAL,), jnp.float32) ** levels(keys[14], (TOKEN_TOTAL,), ((0, 512),), -0.2, 0.2), -14.0, -6.0),
        "rollout_for_segment": jnp.searchsorted(jnp.cumsum(uneven(keys[15], SEQS, BLOCKS, MOST_BLK, 2)), jnp.arange(BLOCKS), side="right").astype(jnp.int32),
        "query_text_for_rollout": set_ends(jax.random.randint(keys[16], (SEQS,), 0, PROMPTS), jax.random.fold_in(keys[16], 1), 0, PROMPTS - 1).astype(jnp.int32),
    }


def reference(acceptance_vector, lookup_vector_array, payload_vector_array, raw_gating_signal, raw_forgetting_rate, current_reward_vector, memory_following_query, group_layernorm_scaling, closing_layernorm_scaling, skip_stream_input, closing_projection, vocabulary_readout, following_labels, response_indicator, baseline_logarithmic_likelihood, rollout_for_segment, query_text_for_rollout):

    def heads_of(a):
        return a.astype(jnp.float32).reshape(TOKEN_TOTAL, ATTENTION_GROUPS, GROUP_DIMENSION)
    inherited_memory = heads_of(acceptance_vector)
    lookup_vectors = heads_of(lookup_vector_array)
    vals = heads_of(payload_vector_array)
    decay = jnp.exp(-jnp.exp(heads_of(raw_forgetting_rate)))
    group_current_reward = current_reward_vector.reshape(ATTENTION_GROUPS, GROUP_DIMENSION)
    prev_seq = jnp.concatenate([jnp.array([-1], jnp.int32), rollout_for_segment[:-1].astype(jnp.int32)])
    block_first = rollout_for_segment != prev_seq
    position = jnp.arange(TOKEN_TOTAL, dtype=jnp.int32)
    block_of = position // TOK_BLK
    tok_first = jnp.logical_and(position % TOK_BLK == 0, block_first[block_of])
    tok_seq = rollout_for_segment[block_of]
    tok_prompt = query_text_for_rollout[tok_seq]
    prompts = memory_following_query.astype(jnp.float32).reshape(PROMPTS, ATTENTION_GROUPS, GROUP_DIMENSION, GROUP_DIMENSION)

    def advance(state, item):
        r_t, current_lookup_vector, current_payload_vector, w_t, first, which = item
        state = jnp.where(first, prompts[which], state)
        extra_piece_term = (group_current_reward * current_lookup_vector)[:, :, None] * current_payload_vector[:, None, :]
        out = jnp.einsum('hi,hij->hj', r_t, state + extra_piece_term, precision=lax.Precision.HIGHEST)
        state = w_t[:, :, None] * state + current_lookup_vector[:, :, None] * current_payload_vector[:, None, :]
        return (state, out)
    start = jnp.zeros((ATTENTION_GROUPS, GROUP_DIMENSION, GROUP_DIMENSION), jnp.float32)
    _, wkv = lax.scan(advance, start, (inherited_memory, lookup_vectors, vals, decay, tok_first, tok_prompt))
    mean = lax.optimization_barrier(jnp.mean(wkv, axis=-1, keepdims=True))
    var = lax.optimization_barrier(jnp.mean((wkv - mean) ** 2, axis=-1, keepdims=True))
    normal_h = (wkv - mean) / jnp.sqrt(var + 0.00064)
    normal_h = normal_h.reshape(TOKEN_TOTAL, EMBED_DIMENSION) * group_layernorm_scaling
    gate = raw_gating_signal.astype(jnp.float32)
    mixed = (normal_h * jax.nn.silu(gate)).astype(jnp.bfloat16)
    hidden = skip_stream_input.astype(jnp.float32) + jnp.dot(mixed, closing_projection, preferred_element_type=jnp.float32)
    hmean = lax.optimization_barrier(jnp.mean(hidden, axis=-1, keepdims=True))
    hvar = lax.optimization_barrier(jnp.mean((hidden - hmean) ** 2, axis=-1, keepdims=True))
    normed = ((hidden - hmean) / jnp.sqrt(hvar + 1e-05) * closing_layernorm_scaling).astype(jnp.bfloat16)
    group = 256
    blocks_n = normed.reshape(TOKEN_TOTAL // group, group, EMBED_DIMENSION)
    blocks_t = following_labels.reshape(TOKEN_TOTAL // group, group)

    def score(item):
        rows_n, rows_t = item
        logits = lax.dot_general(rows_n, vocabulary_readout, (((1,), (1,)), ((), ())), preferred_element_type=jnp.float32)
        top = lax.optimization_barrier(jnp.max(logits, axis=1))
        lse = top + jnp.log(lax.optimization_barrier(jnp.sum(jnp.exp(logits - top[:, None]), axis=1)))
        picked = jnp.take_along_axis(logits, rows_t[:, None].astype(jnp.int32), axis=1)[:, 0]
        return picked - lse
    logp = lax.map(score, (blocks_n, blocks_t)).reshape(TOKEN_TOTAL)
    token_ratio = response_indicator.astype(jnp.float32) * (logp - baseline_logarithmic_likelihood)
    onehot = (jnp.arange(SEQS, dtype=jnp.int32)[:, None] == tok_seq[None, :]).astype(jnp.float32)
    seq_ratio = lax.optimization_barrier(jnp.sum(onehot * token_ratio[None, :], axis=1)) / TOK_BLK
    return (token_ratio, seq_ratio)
```

```python
import functools

import jax
import jax.numpy as jnp
from jax import lax
from jax.experimental import pallas as pl
from jax.experimental.pallas import tpu as pltpu
from jax.sharding import Mesh
from jax.sharding import PartitionSpec as P

CHAN = 64
LANES = 128
TOK_BLK = 128
SUB = 32
F32 = jnp.float32
BF16 = jnp.bfloat16


def parts2(a):
    high = a.astype(BF16)
    return high, (a - high.astype(F32)).astype(BF16)


def parts3(a):
    high, rest = a.astype(BF16), None
    rest = a - high.astype(F32)
    mid = rest.astype(BF16)
    return high, mid, (rest - mid.astype(F32)).astype(BF16)


def mm(a, b):
    return jnp.dot(a, b, preferred_element_type=F32)


def mm_t(a, b):
    return lax.dot_general(a, b, (((1,), (1,)), ((), ())), preferred_element_type=F32)


def running_log_decay(rate):
    log_decay = -jnp.exp(rate.astype(F32))
    rows = log_decay.shape[0]
    i = lax.broadcasted_iota(jnp.int32, (rows, rows), 0)
    j = lax.broadcasted_iota(jnp.int32, (rows, rows), 1)
    lower = (i >= j).astype(F32).astype(BF16)
    total = mm(
        jnp.concatenate([lower] * 3, axis=1), jnp.concatenate(parts3(log_decay), axis=0)
    )
    return log_decay, total


def left_lanes(rows):
    return lax.broadcasted_iota(jnp.int32, (rows, LANES), 1) < CHAN


def block_end_kernel(chunk_rows, k_ref, v_ref, w_ref, out_ref):
    _, inclusive = running_log_decay(w_ref[...])
    last = inclusive[TOK_BLK - 1 :, :]
    late = k_ref[...].astype(F32) * jnp.exp(last - inclusive)
    high, low = parts2(late.T)
    v = v_ref[...]
    both = mm(jnp.concatenate([high, low], axis=1), jnp.concatenate([v, v], axis=0))
    fall = jnp.exp(jnp.broadcast_to(last, (LANES, LANES)).T)
    left = left_lanes(CHAN)
    both = jnp.where(left, both[:CHAN], both[CHAN:])
    fall = jnp.where(left, fall[:CHAN], fall[CHAN:])
    for q in range(CHAN // chunk_rows):
        rows = slice(q * chunk_rows, (q + 1) * chunk_rows)
        out_ref[q, :chunk_rows, :] = both[rows]
        out_ref[q, chunk_rows:, :] = fall[rows]


def relay_kernel(chunk_rows, meta_ref, moved_ref, prompt_ref, out_ref):
    def step(b, state):
        prompt = jnp.where(meta_ref[1, b] == 0, prompt_ref[0], prompt_ref[1])
        state = jnp.where(meta_ref[0, b] != 0, prompt, state)
        out_ref[b] = state
        return moved_ref[b, chunk_rows:, :] * state + moved_ref[b, :chunk_rows, :]

    lax.fori_loop(
        0, moved_ref.shape[0], step, jnp.zeros((chunk_rows, LANES), F32), unroll=8
    )


def mix_kernel(r_ref, k_ref, v_ref, w_ref, g_ref, u_ref, scale_ref, state_ref, out_ref):
    r = r_ref[...].astype(F32)
    k = k_ref[...].astype(F32)
    v = v_ref[...]
    log_decay, inclusive = running_log_decay(w_ref[...])
    exclusive = inclusive - log_decay
    left = left_lanes(SUB)
    pieces = []
    for sub in range(TOK_BLK // SUB):
        a, b = sub * SUB, (sub + 1) * SUB
        pivot = inclusive[a + SUB // 2 - 1 : a + SUB // 2, :]
        rs = r[a:b] * jnp.exp(exclusive[a:b] - pivot)
        ks = k[:b] * jnp.exp(pivot - inclusive[:b])
        rs = jnp.concatenate([jnp.where(left, rs, 0.0), jnp.where(left, 0.0, rs)], axis=0)
        rh, rl = parts2(rs)
        kh, kl = parts2(ks)
        scores = mm_t(
            jnp.concatenate([rh, rl, rh], axis=1), jnp.concatenate([kh, kh, kl], axis=1)
        )
        t = lax.broadcasted_iota(jnp.int32, scores.shape, 0) % SUB + a
        s = lax.broadcasted_iota(jnp.int32, scores.shape, 1)
        sh, sl = parts2(jnp.where(s < t, scores, 0.0))
        both = mm(sh, v[:b]) + mm(sl, v[:b])
        pieces.append(jnp.where(left, both[:SUB], both[SUB:]))
    wkv = jnp.concatenate(pieces, axis=0)
    i = lax.broadcasted_iota(jnp.int32, (LANES, LANES), 0) // CHAN
    j = lax.broadcasted_iota(jnp.int32, (LANES, LANES), 1) // CHAN
    same = (i == j).astype(F32)
    ones = jnp.concatenate([same.astype(BF16)] * 2, axis=0)
    mean_of = jnp.concatenate([(same / CHAN).astype(BF16)] * 2, axis=0)
    now = mm(jnp.concatenate(parts2(r * k * u_ref[...]), axis=1), ones)
    wkv = wkv + now * v.astype(F32)
    state = state_ref[...]
    left = left_lanes(CHAN)
    state = jnp.concatenate([jnp.where(left, state, 0.0), jnp.where(left, 0.0, state)], axis=0)
    rh, rl = parts2(r * jnp.exp(exclusive))
    sh, sl = parts2(state)
    wkv = wkv + mm(
        jnp.concatenate([rh, rl, rh], axis=1), jnp.concatenate([sh, sh, sl], axis=0)
    )
    mean = mm(jnp.concatenate(parts2(wkv), axis=1), mean_of)
    off = wkv - mean
    var = mm(jnp.concatenate(parts2(off * off), axis=1), mean_of)
    g = g_ref[...].astype(F32)
    y = off / jnp.sqrt(var + 0.00064) * scale_ref[...]
    out_ref[...] = (y * (g / (1.0 + jnp.exp(-g)))).astype(out_ref.dtype)


def cost(flops, nbytes):
    return pl.CostEstimate(flops=flops, bytes_accessed=nbytes, transcendentals=0)


def shifted(value, axis, steps):
    count = lax.axis_size(axis)
    return lax.ppermute(value, axis, [(i, (i + steps) % count) for i in range(count)])


def per_device(
    acceptance_vector,
    lookup_vector_array,
    payload_vector_array,
    raw_gating_signal,
    raw_forgetting_rate,
    current_reward_vector,
    memory_following_query,
    group_layernorm_scaling,
    closing_layernorm_scaling,
    skip_stream_input,
    closing_projection,
    vocabulary_readout,
    following_labels,
    response_indicator,
    baseline_logarithmic_likelihood,
    rollout_for_segment,
    query_text_for_rollout,
):
    nx, nz, ny, nc = (lax.axis_size(a) for a in ("x", "z", "y", "c"))
    ix, iz, iy, ic = (lax.axis_index(a) for a in ("x", "z", "y", "c"))
    n_blk, n_head = nx * nz, ny * nc
    blk, head = ix * nz + iz, iy * nc + ic
    rows, width = acceptance_vector.shape
    embed = skip_stream_input.shape[1]
    pairs = width // LANES
    own = rows // n_head

    proj = lax.all_gather(closing_projection, "z", axis=1, tiled=True)
    share = vocabulary_readout.shape[0] // n_head
    vocab_share = lax.dynamic_slice_in_dim(vocabulary_readout, head * share, share)

    chunks = n_blk // pairs
    chunk_rows = CHAN // chunks
    col = pl.BlockSpec((rows, LANES), lambda p: (0, p))
    end = pl.pallas_call(
        functools.partial(block_end_kernel, chunk_rows),
        grid=(pairs,),
        in_specs=[col] * 3,
        out_specs=pl.BlockSpec((chunks, 2 * chunk_rows, LANES), lambda p: (p, 0, 0)),
        out_shape=jax.ShapeDtypeStruct((n_blk, 2 * chunk_rows, LANES), F32),
        cost_estimate=cost(pairs * 20_000_000, 3 * rows * width * 2),
    )(lookup_vector_array, payload_vector_array, raw_forgetting_rate)
    moved = lax.all_to_all(end, ("x", "z"), 0, 0, tiled=True)

    prev_seq = jnp.concatenate([jnp.full((1,), -1, jnp.int32), rollout_for_segment[:-1]])
    starts = (rollout_for_segment != prev_seq).astype(jnp.int32)
    meta = jnp.stack([starts, query_text_for_rollout[rollout_for_segment]])
    prompts = memory_following_query.shape[0]
    prompt = lax.dynamic_slice(
        memory_following_query.reshape(prompts, pairs, 2, CHAN, CHAN),
        (0, blk // chunks, 0, (blk % chunks) * chunk_rows, 0),
        (prompts, 1, 2, chunk_rows, CHAN),
    )[:, 0]
    prompt = prompt.transpose(0, 2, 1, 3).reshape(prompts, chunk_rows, LANES).astype(F32)
    vmem = pl.BlockSpec(memory_space=pltpu.VMEM)
    entering = pl.pallas_call(
        functools.partial(relay_kernel, chunk_rows),
        in_specs=[pl.BlockSpec(memory_space=pltpu.SMEM), vmem, vmem],
        out_specs=vmem,
        out_shape=jax.ShapeDtypeStruct((n_blk, chunk_rows, LANES), F32),
        cost_estimate=cost(1_000_000, 500_000),
    )(meta, moved, prompt)
    entering = lax.all_to_all(entering, ("x", "z"), 0, 0, tiled=True)
    entering = entering.reshape(pairs * CHAN, LANES)

    row = pl.BlockSpec((1, LANES), lambda p: (0, p))
    mixed = pl.pallas_call(
        mix_kernel,
        grid=(pairs,),
        in_specs=[col] * 5 + [row] * 2 + [pl.BlockSpec((CHAN, LANES), lambda p: (p, 0))],
        out_specs=col,
        out_shape=jax.ShapeDtypeStruct((rows, width), BF16),
        cost_estimate=cost(pairs * 60_000_000, 6 * rows * width * 2),
    )(
        acceptance_vector,
        lookup_vector_array,
        payload_vector_array,
        raw_forgetting_rate,
        raw_gating_signal,
        current_reward_vector[None, :],
        group_layernorm_scaling[None, :],
        entering,
    )

    mixed = lax.all_gather(mixed, "x", axis=0)
    mixed = mixed.reshape(nx, ny, nc, own, width).transpose(2, 1, 0, 3, 4)
    mixed = mixed.reshape(nc, ny * nx * own, width)
    theirs = mm(lax.dynamic_index_in_dim(mixed, 1 - ic, 0, False), proj)
    mine = mm(lax.dynamic_index_in_dim(mixed, ic, 0, False), proj)
    partial = mine + shifted(theirs, "c", 1)
    partial = partial.reshape(ny * nx, own, embed // nx)
    partial = lax.all_to_all(partial, ("y", "x"), 0, 0, tiled=True)
    projected = jnp.sum(partial.reshape(ny, nx, own, embed // nx), axis=0)
    projected = projected.transpose(1, 0, 2).reshape(own, embed)
    hidden = skip_stream_input.astype(F32) + projected
    hmean = jnp.mean(hidden, axis=-1, keepdims=True)
    hvar = jnp.mean((hidden - hmean) ** 2, axis=-1, keepdims=True)
    normed = ((hidden - hmean) / jnp.sqrt(hvar + 1e-05) * closing_layernorm_scaling).astype(BF16)

    tokens = lax.all_gather(normed, "y", axis=0, tiled=True)
    tokens = jnp.concatenate([tokens] + [shifted(tokens, "x", s) for s in range(1, nx)], axis=0)
    other = shifted(tokens, "c", 1)
    vocab_rows = lax.all_gather(vocab_share, "z", axis=0, tiled=True)

    facts = jnp.stack(
        [
            following_labels.astype(F32),
            response_indicator.astype(F32),
            baseline_logarithmic_likelihood,
        ]
    )
    facts, _ = lax.optimization_barrier((facts, other))
    facts = lax.all_gather(facts, ("x", "y", "c"), axis=0)
    facts = facts.reshape(nx, ny, nc, 3, own).transpose(3, 2, 0, 1, 4)
    labels = facts[0].astype(jnp.int32)
    back = (ix - jnp.arange(nx)) % nx

    index = jnp.arange(nz * share, dtype=jnp.int32)
    vocab_local = vocabulary_readout.shape[0]
    entry = (ix * nz + index // share) * vocab_local + head * share + index % share

    def score(toks, core):
        logits = mm_t(toks, vocab_rows)
        top = jnp.max(logits, axis=1)
        total = jnp.sum(jnp.exp(logits - top[:, None]), axis=1)
        wanted = lax.dynamic_index_in_dim(labels, core, 0, False)[back].reshape(-1)
        picked = jnp.sum(jnp.where(entry[None, :] == wanted[:, None], logits, 0.0), axis=1)
        both = jnp.stack([top + jnp.log(total), picked])
        return both.reshape(2, nx, ny * own)[:, back]

    first, second = score(tokens, ic), score(other, 1 - ic)
    both = jnp.where(
        ic == 0, jnp.stack([first, second], axis=1), jnp.stack([second, first], axis=1)
    )
    plane = nx * ny * nc
    count = plane * own
    both = jnp.broadcast_to(both.reshape(1, 2 * count // LANES, LANES), (plane, 2 * count // LANES, LANES))
    both = lax.all_to_all(both, ("x", "y", "c"), 0, 0, tiled=True).reshape(plane, 2, count)
    part, picked = both[:, 0], both[:, 1]
    peak = jnp.max(part, axis=0)
    logp = jnp.sum(picked, axis=0) - peak - jnp.log(jnp.sum(jnp.exp(part - peak), axis=0))
    ratio = facts[1] * (logp.reshape(nc, nx, ny, own) - facts[2])
    token_ratio = lax.dynamic_slice(ratio, (ic, ix, iy, 0), (1, 1, 1, own)).reshape(own)

    sums = jnp.sum(ratio, axis=(0, 2, 3))
    sums = jnp.broadcast_to(jnp.pad(sums, (0, LANES - nx)), (nz, 1, LANES))
    sums = lax.all_to_all(sums, "z", 0, 0, tiled=True)[:, 0, :nx]
    seq_of = rollout_for_segment.reshape(nx, nz).T
    marker = jnp.arange(query_text_for_rollout.shape[0])[:, None, None] == seq_of[None]
    seq_ratio = jnp.sum(jnp.where(marker, sums[None], 0.0), axis=(1, 2)) / TOK_BLK
    return (token_ratio, seq_ratio)


def solution(mesh):
    n_blk, n_head = mesh.devices.shape
    nx, nc = 4, 2
    fine = Mesh(
        mesh.devices.reshape(nx, n_blk // nx, n_head // nc, nc), ("x", "z", "y", "c")
    )
    blk, head = ("x", "z"), ("y", "c")
    placed = (
        P(blk, head),
        P(blk, head),
        P(blk, head),
        P(blk, head),
        P(blk, head),
        P(head),
        P(None, head, None),
        P(head),
        P(),
        P(blk + head, None),
        P(head, blk),
        P(blk, None),
        P(blk + head),
        P(blk + head),
        P(blk + head),
        P(),
        P(),
    )
    return jax.shard_map(
        per_device, mesh=fine, in_specs=placed, out_specs=(P(blk + head), P()), check_vma=False
    )
```

```python
import functools

import jax
import jax.numpy as jnp
from jax import lax
from jax.experimental import pallas as pl
from jax.experimental.pallas import tpu as pltpu
from jax.sharding import Mesh
from jax.sharding import PartitionSpec as P

CHAN = 64
LANES = 128
TOK_BLK = 128
SUB = 32
F32 = jnp.float32
BF16 = jnp.bfloat16


def parts2(a):
    high = a.astype(BF16)
    return high, (a - high.astype(F32)).astype(BF16)


def parts3(a):
    high, rest = a.astype(BF16), None
    rest = a - high.astype(F32)
    mid = rest.astype(BF16)
    return high, mid, (rest - mid.astype(F32)).astype(BF16)


def mm(a, b):
    return jnp.dot(a, b, preferred_element_type=F32)


def mm_t(a, b):
    return lax.dot_general(a, b, (((1,), (1,)), ((), ())), preferred_element_type=F32)


def running_log_decay(rate):
    log_decay = -jnp.exp(rate.astype(F32))
    rows = log_decay.shape[0]
    i = lax.broadcasted_iota(jnp.int32, (rows, rows), 0)
    j = lax.broadcasted_iota(jnp.int32, (rows, rows), 1)
    lower = (i >= j).astype(F32).astype(BF16)
    total = mm(
        jnp.concatenate([lower] * 3, axis=1), jnp.concatenate(parts3(log_decay), axis=0)
    )
    return log_decay, total


def left_lanes(rows):
    return lax.broadcasted_iota(jnp.int32, (rows, LANES), 1) < CHAN


def block_end_kernel(chunk_rows, k_ref, v_ref, w_ref, out_ref):
    _, inclusive = running_log_decay(w_ref[...])
    last = inclusive[TOK_BLK - 1 :, :]
    late = k_ref[...].astype(F32) * jnp.exp(last - inclusive)
    high, low = parts2(late.T)
    v = v_ref[...]
    both = mm(jnp.concatenate([high, low], axis=1), jnp.concatenate([v, v], axis=0))
    fall = jnp.exp(jnp.broadcast_to(last, (LANES, LANES)).T)
    left = left_lanes(CHAN)
    both = jnp.where(left, both[:CHAN], both[CHAN:])
    fall = jnp.where(left, fall[:CHAN], fall[CHAN:])
    for q in range(CHAN // chunk_rows):
        rows = slice(q * chunk_rows, (q + 1) * chunk_rows)
        out_ref[q, :chunk_rows, :] = both[rows]
        out_ref[q, chunk_rows:, :] = fall[rows]


def relay_kernel(chunk_rows, meta_ref, moved_ref, prompt_ref, out_ref):
    def step(b, state):
        prompt = jnp.where(meta_ref[1, b] == 0, prompt_ref[0], prompt_ref[1])
        state = jnp.where(meta_ref[0, b] != 0, prompt, state)
        out_ref[b] = state
        return moved_ref[b, chunk_rows:, :] * state + moved_ref[b, :chunk_rows, :]

    lax.fori_loop(
        0, moved_ref.shape[0], step, jnp.zeros((chunk_rows, LANES), F32), unroll=8
    )


def within_kernel(r_ref, k_ref, v_ref, w_ref, u_ref, wkv_ref, high_ref, low_ref):
    r = r_ref[...].astype(F32)
    k = k_ref[...].astype(F32)
    v = v_ref[...]
    log_decay, inclusive = running_log_decay(w_ref[...])
    exclusive = inclusive - log_decay
    left = left_lanes(SUB)
    pieces = []
    for sub in range(TOK_BLK // SUB):
        a, b = sub * SUB, (sub + 1) * SUB
        pivot = inclusive[a + SUB // 2 - 1 : a + SUB // 2, :]
        rs = r[a:b] * jnp.exp(exclusive[a:b] - pivot)
        ks = k[:b] * jnp.exp(pivot - inclusive[:b])
        rs = jnp.concatenate([jnp.where(left, rs, 0.0), jnp.where(left, 0.0, rs)], axis=0)
        rh, rl = parts2(rs)
        kh, kl = parts2(ks)
        scores = mm_t(
            jnp.concatenate([rh, rl, rh], axis=1), jnp.concatenate([kh, kh, kl], axis=1)
        )
        t = lax.broadcasted_iota(jnp.int32, scores.shape, 0) % SUB + a
        s = lax.broadcasted_iota(jnp.int32, scores.shape, 1)
        sh, sl = parts2(jnp.where(s < t, scores, 0.0))
        both = mm(sh, v[:b]) + mm(sl, v[:b])
        pieces.append(jnp.where(left, both[:SUB], both[SUB:]))
    now = mm(jnp.concatenate(parts2(r * k * u_ref[...]), axis=1), same_head(1.0))
    wkv_ref[...] = jnp.concatenate(pieces, axis=0) + now * v.astype(F32)
    high_ref[...], low_ref[...] = parts2(r * jnp.exp(exclusive))


def same_head(value):
    i = lax.broadcasted_iota(jnp.int32, (LANES, LANES), 0) // CHAN
    j = lax.broadcasted_iota(jnp.int32, (LANES, LANES), 1) // CHAN
    return jnp.concatenate([jnp.where(i == j, value, 0.0).astype(BF16)] * 2, axis=0)


def mix_kernel(wkv_ref, high_ref, low_ref, g_ref, scale_ref, state_ref, out_ref):
    state = state_ref[...]
    left = left_lanes(CHAN)
    state = jnp.concatenate([jnp.where(left, state, 0.0), jnp.where(left, 0.0, state)], axis=0)
    sh, sl = parts2(state)
    high = high_ref[...]
    wkv = wkv_ref[...] + mm(
        jnp.concatenate([high, low_ref[...], high], axis=1), jnp.concatenate([sh, sh, sl], axis=0)
    )
    mean_of = same_head(1.0 / CHAN)
    mean = mm(jnp.concatenate(parts2(wkv), axis=1), mean_of)
    off = wkv - mean
    var = mm(jnp.concatenate(parts2(off * off), axis=1), mean_of)
    g = g_ref[...].astype(F32)
    y = off / jnp.sqrt(var + 0.00064) * scale_ref[...]
    out_ref[...] = (y * (g / (1.0 + jnp.exp(-g)))).astype(out_ref.dtype)


def score_kernel(share_bits, vocab_bits, place_ref, mine_ref, theirs_ref, label_ref, vocab_ref, out_ref, top_ref, sum_ref, pick_ref):
    step = pl.program_id(0)
    tile, half = vocab_ref.shape[0], mine_ref.shape[0]
    core = place_ref[0]

    @pl.when(step == 0)
    def _():
        top_ref[...] = jnp.full_like(top_ref, -3.0e38)
        sum_ref[...] = jnp.zeros_like(sum_ref)
        pick_ref[...] = jnp.zeros_like(pick_ref)

    index = step * tile + lax.broadcasted_iota(jnp.int32, (tile, half), 0)
    group = lax.shift_right_logical(index, share_bits)
    entry = place_ref[1] + lax.shift_left(group, vocab_bits) + (index & ((1 << share_bits) - 1))
    for part, tokens in enumerate((mine_ref, theirs_ref)):
        at = slice(part * half, (part + 1) * half)
        label = jnp.where(core == part, label_ref[:, :half], label_ref[:, half:])
        logits = mm_t(vocab_ref[...], tokens[...])
        old = top_ref[:, at]
        top = jnp.maximum(old, jnp.max(logits, axis=0, keepdims=True))
        fresh = jnp.sum(jnp.exp(logits - top), axis=0, keepdims=True)
        sum_ref[:, at] = sum_ref[:, at] * jnp.exp(old - top) + fresh
        pick_ref[:, at] += jnp.sum(jnp.where(entry == label, logits, 0.0), axis=0, keepdims=True)
        top_ref[:, at] = top

    @pl.when(step == pl.num_programs(0) - 1)
    def _():
        part = top_ref[...] + jnp.log(sum_ref[...])
        for row, value in enumerate((part, pick_ref[...])):
            first, second = value[:, :half], value[:, half:]
            out_ref[row : row + 1, :half] = jnp.where(core == 0, first, second)
            out_ref[row : row + 1, half:] = jnp.where(core == 0, second, first)


def cost(flops, nbytes):
    return pl.CostEstimate(flops=flops, bytes_accessed=nbytes, transcendentals=0)


def shifted(value, axis, steps):
    count = lax.axis_size(axis)
    return lax.ppermute(value, axis, [(i, (i + steps) % count) for i in range(count)])


def copies(value, axes):
    count = lax.axis_size(axes)
    sent = jnp.broadcast_to(value[None], (count, *value.shape))
    return lax.all_to_all(sent, axes, 0, 0, tiled=True)


def spread(value, axis, groups):
    count = len(groups[0])
    place = sum(
        jnp.where(lax.axis_index(axis) == source, i, 0)
        for group in groups
        for i, source in enumerate(group)
    )
    out = jnp.zeros((count, *value.shape), value.dtype)
    for step in range(count):
        pairs = [(g[i], g[(i + step) % count]) for g in groups for i in range(count)]
        piece = lax.ppermute(value, axis, pairs) if step else value
        out = lax.dynamic_update_index_in_dim(out, piece, (place - step) % count, 0)
    return out


def per_device(
    acceptance_vector,
    lookup_vector_array,
    payload_vector_array,
    raw_gating_signal,
    raw_forgetting_rate,
    current_reward_vector,
    memory_following_query,
    group_layernorm_scaling,
    closing_layernorm_scaling,
    skip_stream_input,
    closing_projection,
    vocabulary_readout,
    following_labels,
    response_indicator,
    baseline_logarithmic_likelihood,
    rollout_for_segment,
    query_text_for_rollout,
):
    nx, nz, ny, nc = (lax.axis_size(a) for a in ("x", "z", "y", "c"))
    ix, iz, iy, ic = (lax.axis_index(a) for a in ("x", "z", "y", "c"))
    n_blk, n_head = nx * nz, ny * nc
    blk, head = ix * nz + iz, iy * nc + ic
    rows, width = acceptance_vector.shape
    embed = skip_stream_input.shape[1]
    pairs = width // LANES
    own = rows // n_head

    vocab_local = vocabulary_readout.shape[0]
    share = vocab_local // n_head
    vocab_share = lax.dynamic_slice_in_dim(vocabulary_readout, head * share, share)
    vocab_rows = lax.all_gather(vocab_share, "z", axis=0, tiled=True)

    chunks = n_blk // pairs
    chunk_rows = CHAN // chunks
    col = pl.BlockSpec((rows, LANES), lambda p: (0, p))
    end = pl.pallas_call(
        functools.partial(block_end_kernel, chunk_rows),
        grid=(pairs,),
        in_specs=[col] * 3,
        out_specs=pl.BlockSpec((chunks, 2 * chunk_rows, LANES), lambda p: (p, 0, 0)),
        out_shape=jax.ShapeDtypeStruct((n_blk, 2 * chunk_rows, LANES), F32),
        cost_estimate=cost(pairs * 20_000_000, 3 * rows * width * 2),
    )(lookup_vector_array, payload_vector_array, raw_forgetting_rate)
    moved = lax.all_to_all(end, ("x", "z"), 0, 0, tiled=True)

    columns, facts, bonus, _ = lax.optimization_barrier(
        (
            closing_projection.T,
            jnp.concatenate(
                [
                    following_labels.astype(F32),
                    response_indicator.astype(F32),
                    baseline_logarithmic_likelihood,
                ]
            ),
            current_reward_vector[None, :],
            end,
        )
    )
    far = [[i + j * 4 for j in range(nz // 4)] for i in range(4)]
    near = [[i * 4 + j for j in range(4)] for i in range(nz // 4)]
    columns = spread(columns, "z", far)
    plane = nx * ny * nc
    facts = jnp.pad(facts, (0, LANES - 3 * own)).reshape(1, LANES)
    facts = spread(facts, "c", [list(range(nc))])
    row = pl.BlockSpec((1, LANES), lambda p: (0, p))
    within, high, low = pl.pallas_call(
        within_kernel,
        grid=(pairs,),
        in_specs=[col] * 4 + [row],
        out_specs=[col] * 3,
        out_shape=[jax.ShapeDtypeStruct((rows, width), t) for t in (F32, BF16, BF16)],
        cost_estimate=cost(pairs * 60_000_000, 8 * rows * width * 2),
    )(acceptance_vector, lookup_vector_array, payload_vector_array, raw_forgetting_rate, bonus)

    moved, within, high, low, columns, facts = lax.optimization_barrier(
        (moved, within, high, low, columns, facts)
    )
    prev_seq = jnp.concatenate([jnp.full((1,), -1, jnp.int32), rollout_for_segment[:-1]])
    starts = (rollout_for_segment != prev_seq).astype(jnp.int32)
    meta = jnp.stack([starts, query_text_for_rollout[rollout_for_segment]])
    prompts = memory_following_query.shape[0]
    prompt = lax.dynamic_slice(
        memory_following_query.reshape(prompts, pairs, 2, CHAN, CHAN),
        (0, blk // chunks, 0, (blk % chunks) * chunk_rows, 0),
        (prompts, 1, 2, chunk_rows, CHAN),
    )[:, 0]
    prompt = prompt.transpose(0, 2, 1, 3).reshape(prompts, chunk_rows, LANES).astype(F32)
    vmem = pl.BlockSpec(memory_space=pltpu.VMEM)
    entering = pl.pallas_call(
        functools.partial(relay_kernel, chunk_rows),
        in_specs=[pl.BlockSpec(memory_space=pltpu.SMEM), vmem, vmem],
        out_specs=vmem,
        out_shape=jax.ShapeDtypeStruct((n_blk, chunk_rows, LANES), F32),
        cost_estimate=cost(1_000_000, 500_000),
    )(meta, moved, prompt)
    columns, facts, _ = lax.optimization_barrier((columns, facts, entering))
    entering = lax.all_to_all(entering, ("x", "z"), 0, 0, tiled=True)
    columns = spread(columns, "z", near).transpose(1, 0, 2, 3).reshape(-1, width)
    facts = spread(facts, "y", [list(range(ny))])
    entering, facts = lax.optimization_barrier((entering, facts))
    entering = entering.reshape(pairs * CHAN, LANES)

    mixed = pl.pallas_call(
        mix_kernel,
        grid=(pairs,),
        in_specs=[col] * 4 + [row, pl.BlockSpec((CHAN, LANES), lambda p: (p, 0))],
        out_specs=col,
        out_shape=jax.ShapeDtypeStruct((rows, width), BF16),
        cost_estimate=cost(pairs * 20_000_000, 6 * rows * width * 2),
    )(within, high, low, raw_gating_signal, group_layernorm_scaling[None, :], entering)

    mixed = lax.all_gather(mixed, "x", axis=0)
    mixed = mixed.reshape(nx, ny, nc, own, width).transpose(2, 1, 0, 3, 4)
    mixed = mixed.reshape(nc, ny * nx * own, width)
    theirs = mm_t(lax.dynamic_index_in_dim(mixed, 1 - ic, 0, False), columns)
    mine = mm_t(lax.dynamic_index_in_dim(mixed, ic, 0, False), columns)
    partial = mine + shifted(theirs, "c", 1)
    partial = partial.reshape(ny * nx, own, embed // nx)
    partial, facts = lax.optimization_barrier((partial, facts))
    facts = spread(facts, "x", [list(range(nx))])
    partial = lax.all_to_all(partial, ("y", "x"), 0, 0, tiled=True)
    projected = jnp.sum(partial.reshape(ny, nx, own, embed // nx), axis=0)
    projected = projected.transpose(1, 0, 2).reshape(own, embed)
    hidden = skip_stream_input.astype(F32) + projected
    hmean = jnp.mean(hidden, axis=-1, keepdims=True)
    hvar = jnp.mean((hidden - hmean) ** 2, axis=-1, keepdims=True)
    normed = ((hidden - hmean) / jnp.sqrt(hvar + 1e-05) * closing_layernorm_scaling).astype(BF16)

    normed, facts = lax.optimization_barrier((normed, facts))
    facts = facts[..., 0, : 3 * own].reshape(nx, ny, nc, 3, own).transpose(3, 2, 1, 0, 4)

    tokens = copies(normed, ("y", "x")).reshape(ny * nx * own, embed)
    other = shifted(tokens, "c", 1)
    count = plane * own
    labels = facts[0].reshape(1, count).astype(jnp.int32)
    tile = min(256, nz * share)
    place = jnp.stack([ic, ix * nz * vocab_local + head * share]).astype(jnp.int32)
    whole = lambda *shape: pl.BlockSpec(shape, lambda i: (0,) * len(shape))
    both = pl.pallas_call(
        functools.partial(score_kernel, share.bit_length() - 1, vocab_local.bit_length() - 1),
        grid=(nz * share // tile,),
        in_specs=[
            pl.BlockSpec(memory_space=pltpu.SMEM),
            whole(count // nc, embed),
            whole(count // nc, embed),
            whole(1, count),
            pl.BlockSpec((tile, embed), lambda i: (i, 0)),
        ],
        out_specs=whole(2, count),
        out_shape=jax.ShapeDtypeStruct((2, count), F32),
        scratch_shapes=[pltpu.VMEM((1, count), F32)] * 3,
        compiler_params=pltpu.CompilerParams(vmem_limit_bytes=40 * 1024 * 1024),
        cost_estimate=cost(2 * count * nz * share * embed, (count + nz * share) * embed * 2),
    )(place, tokens, other, labels, vocab_rows)
    both = copies(both, ("x", "y", "c"))
    part, picked = both[:, 0], both[:, 1]
    peak = jnp.max(part, axis=0)
    logp = jnp.sum(picked, axis=0) - peak - jnp.log(jnp.sum(jnp.exp(part - peak), axis=0))
    ratio = facts[1] * (logp.reshape(nc, ny, nx, own) - facts[2])
    token_ratio = lax.dynamic_slice(ratio, (ic, iy, ix, 0), (1, 1, 1, own)).reshape(own)

    sums = jnp.sum(ratio, axis=(0, 1, 3))
    sums = copies(jnp.pad(sums, (0, LANES - nx)).reshape(1, LANES), "z")[:, 0, :nx]
    seq_of = rollout_for_segment.reshape(nx, nz).T
    marker = jnp.arange(query_text_for_rollout.shape[0])[:, None, None] == seq_of[None]
    seq_ratio = jnp.sum(jnp.where(marker, sums[None], 0.0), axis=(1, 2)) / TOK_BLK
    return (token_ratio, seq_ratio)


def solution(mesh):
    n_blk, n_head = mesh.devices.shape
    nx, nc = 4, 2
    fine = Mesh(
        mesh.devices.reshape(nx, n_blk // nx, n_head // nc, nc), ("x", "z", "y", "c")
    )
    blk, head = ("x", "z"), ("y", "c")
    placed = (
        P(blk, head),
        P(blk, head),
        P(blk, head),
        P(blk, head),
        P(blk, head),
        P(head),
        P(None, head, None),
        P(head),
        P(),
        P(blk + head, None),
        P(head, blk),
        P(blk, None),
        P(blk + head),
        P(blk + head),
        P(blk + head),
        P(),
        P(),
    )
    return jax.shard_map(
        per_device, mesh=fine, in_specs=placed, out_specs=(P(blk + head), P()), check_vma=False
    )
```

```python
import functools

import jax
import jax.numpy as jnp
from jax import lax
from jax.experimental import pallas as pl
from jax.experimental.pallas import tpu as pltpu
from jax.sharding import Mesh
from jax.sharding import PartitionSpec as P

CHAN = 64
LANES = 128
TOK_BLK = 128
SUB = 32
F32 = jnp.float32
BF16 = jnp.bfloat16


def parts2(a):
    high = a.astype(BF16)
    return high, (a - high.astype(F32)).astype(BF16)


def parts3(a):
    high, rest = a.astype(BF16), None
    rest = a - high.astype(F32)
    mid = rest.astype(BF16)
    return high, mid, (rest - mid.astype(F32)).astype(BF16)


def mm(a, b):
    return jnp.dot(a, b, preferred_element_type=F32)


def mm_t(a, b):
    return lax.dot_general(a, b, (((1,), (1,)), ((), ())), preferred_element_type=F32)


def running_log_decay(rate):
    log_decay = -jnp.exp(rate.astype(F32))
    rows = log_decay.shape[0]
    i = lax.broadcasted_iota(jnp.int32, (rows, rows), 0)
    j = lax.broadcasted_iota(jnp.int32, (rows, rows), 1)
    lower = (i >= j).astype(F32).astype(BF16)
    total = mm(
        jnp.concatenate([lower] * 3, axis=1), jnp.concatenate(parts3(log_decay), axis=0)
    )
    return log_decay, total


def left_lanes(rows):
    return lax.broadcasted_iota(jnp.int32, (rows, LANES), 1) < CHAN


def block_end_kernel(chunk_rows, k_ref, v_ref, w_ref, out_ref):
    _, inclusive = running_log_decay(w_ref[...])
    last = inclusive[TOK_BLK - 1 :, :]
    late = k_ref[...].astype(F32) * jnp.exp(last - inclusive)
    high, low = parts2(late.T)
    v = v_ref[...]
    both = mm(jnp.concatenate([high, low], axis=1), jnp.concatenate([v, v], axis=0))
    fall = jnp.exp(jnp.broadcast_to(last, (LANES, LANES)).T)
    left = left_lanes(CHAN)
    both = jnp.where(left, both[:CHAN], both[CHAN:])
    fall = jnp.where(left, fall[:CHAN], fall[CHAN:])
    for q in range(CHAN // chunk_rows):
        rows = slice(q * chunk_rows, (q + 1) * chunk_rows)
        out_ref[q, :chunk_rows, :] = both[rows]
        out_ref[q, chunk_rows:, :] = fall[rows]


def relay_kernel(chunk_rows, meta_ref, moved_ref, prompt_ref, out_ref):
    def step(b, state):
        prompt = jnp.where(meta_ref[1, b] == 0, prompt_ref[0], prompt_ref[1])
        state = jnp.where(meta_ref[0, b] != 0, prompt, state)
        out_ref[b] = state
        return moved_ref[b, chunk_rows:, :] * state + moved_ref[b, :chunk_rows, :]

    lax.fori_loop(
        0, moved_ref.shape[0], step, jnp.zeros((chunk_rows, LANES), F32), unroll=8
    )


def within_kernel(r_ref, k_ref, v_ref, w_ref, u_ref, wkv_ref, high_ref, low_ref):
    r = r_ref[...].astype(F32)
    k = k_ref[...].astype(F32)
    v = v_ref[...]
    log_decay, inclusive = running_log_decay(w_ref[...])
    exclusive = inclusive - log_decay
    left = left_lanes(SUB)
    pieces = []
    for sub in range(TOK_BLK // SUB):
        a, b = sub * SUB, (sub + 1) * SUB
        pivot = inclusive[a + SUB // 2 - 1 : a + SUB // 2, :]
        rs = r[a:b] * jnp.exp(exclusive[a:b] - pivot)
        ks = k[:b] * jnp.exp(pivot - inclusive[:b])
        rs = jnp.concatenate([jnp.where(left, rs, 0.0), jnp.where(left, 0.0, rs)], axis=0)
        rh, rl = parts2(rs)
        kh, kl = parts2(ks)
        scores = mm_t(
            jnp.concatenate([rh, rl, rh], axis=1), jnp.concatenate([kh, kh, kl], axis=1)
        )
        t = lax.broadcasted_iota(jnp.int32, scores.shape, 0) % SUB + a
        s = lax.broadcasted_iota(jnp.int32, scores.shape, 1)
        sh, sl = parts2(jnp.where(s < t, scores, 0.0))
        both = mm(sh, v[:b]) + mm(sl, v[:b])
        pieces.append(jnp.where(left, both[:SUB], both[SUB:]))
    now = mm(jnp.concatenate(parts2(r * k * u_ref[...]), axis=1), same_head(1.0))
    wkv_ref[...] = jnp.concatenate(pieces, axis=0) + now * v.astype(F32)
    high_ref[...], low_ref[...] = parts2(r * jnp.exp(exclusive))


def same_head(value):
    i = lax.broadcasted_iota(jnp.int32, (LANES, LANES), 0) // CHAN
    j = lax.broadcasted_iota(jnp.int32, (LANES, LANES), 1) // CHAN
    return jnp.concatenate([jnp.where(i == j, value, 0.0).astype(BF16)] * 2, axis=0)


def mix_kernel(wkv_ref, high_ref, low_ref, g_ref, scale_ref, state_ref, out_ref):
    state = state_ref[...]
    left = left_lanes(CHAN)
    state = jnp.concatenate([jnp.where(left, state, 0.0), jnp.where(left, 0.0, state)], axis=0)
    sh, sl = parts2(state)
    high = high_ref[...]
    wkv = wkv_ref[...] + mm(
        jnp.concatenate([high, low_ref[...], high], axis=1), jnp.concatenate([sh, sh, sl], axis=0)
    )
    mean_of = same_head(1.0 / CHAN)
    mean = mm(jnp.concatenate(parts2(wkv), axis=1), mean_of)
    off = wkv - mean
    var = mm(jnp.concatenate(parts2(off * off), axis=1), mean_of)
    g = g_ref[...].astype(F32)
    y = off / jnp.sqrt(var + 0.00064) * scale_ref[...]
    out_ref[...] = (y * (g / (1.0 + jnp.exp(-g)))).astype(out_ref.dtype)


def score_kernel(
    layout, first, final, place_ref, mine_ref, theirs_ref, label_ref, vocab_ref, *refs
):
    group, skipped, offset, vocab_local = layout
    known_ref, (out_ref, state_ref) = (None, refs) if first else (refs[0], refs[1:])
    step = pl.program_id(0)
    tile, half = vocab_ref.shape[0], mine_ref.shape[0]
    core = place_ref[0]

    @pl.when(step == 0)
    def _():
        if first:
            state_ref[0:1] = jnp.full((1, 2 * half), -3.0e38, F32)
            state_ref[1:3] = jnp.zeros((2, 2 * half), F32)
        else:
            state_ref[...] = known_ref[...]

    index = step * tile + lax.broadcasted_iota(jnp.int32, (tile, 1), 0)
    source = lax.div(index, jnp.int32(group))
    row = index - source * group
    entry = jnp.where(
        row < skipped, -1, place_ref[1] + source * vocab_local + (row - skipped + offset)
    )
    for part, tokens in enumerate((mine_ref, theirs_ref)):
        at = slice(part * half, (part + 1) * half)
        label = jnp.where(core == part, label_ref[:, :half], label_ref[:, half:])
        logits = mm_t(vocab_ref[...], tokens[...])
        found = jnp.where(entry == label, logits, 0.0)
        if skipped:
            logits = jnp.where(entry < 0, -3.0e38, logits)
        old = state_ref[0:1, at]
        top = jnp.maximum(old, jnp.max(logits, axis=0, keepdims=True))
        fresh = jnp.sum(jnp.exp(logits - top), axis=0, keepdims=True)
        state_ref[1:2, at] = state_ref[1:2, at] * jnp.exp(old - top) + fresh
        state_ref[2:3, at] += jnp.sum(found, axis=0, keepdims=True)
        state_ref[0:1, at] = top

    @pl.when(step == pl.num_programs(0) - 1)
    def _():
        if not final:
            out_ref[...] = state_ref[...]
            return
        part = state_ref[0:1] + jnp.log(state_ref[1:2])
        for row, value in enumerate((part, state_ref[2:3])):
            left, right = value[:, :half], value[:, half:]
            out_ref[row : row + 1, :half] = jnp.where(core == 0, left, right)
            out_ref[row : row + 1, half:] = jnp.where(core == 0, right, left)


def cost(flops, nbytes):
    return pl.CostEstimate(flops=flops, bytes_accessed=nbytes, transcendentals=0)


def shifted(value, axis, steps):
    count = lax.axis_size(axis)
    return lax.ppermute(value, axis, [(i, (i + steps) % count) for i in range(count)])


def copies(value, axes):
    count = lax.axis_size(axes)
    sent = jnp.broadcast_to(value[None], (count, *value.shape))
    return lax.all_to_all(sent, axes, 0, 0, tiled=True)


def spread(value, axis, groups):
    count = len(groups[0])
    place = sum(
        jnp.where(lax.axis_index(axis) == source, i, 0)
        for group in groups
        for i, source in enumerate(group)
    )
    out = jnp.zeros((count, *value.shape), value.dtype)
    for step in range(count):
        pairs = [(g[i], g[(i + step) % count]) for g in groups for i in range(count)]
        piece = lax.ppermute(value, axis, pairs) if step else value
        out = lax.dynamic_update_index_in_dim(out, piece, (place - step) % count, 0)
    return out


def per_device(
    acceptance_vector,
    lookup_vector_array,
    payload_vector_array,
    raw_gating_signal,
    raw_forgetting_rate,
    current_reward_vector,
    memory_following_query,
    group_layernorm_scaling,
    closing_layernorm_scaling,
    skip_stream_input,
    closing_projection,
    vocabulary_readout,
    following_labels,
    response_indicator,
    baseline_logarithmic_likelihood,
    rollout_for_segment,
    query_text_for_rollout,
):
    nx, nz, ny, nc = (lax.axis_size(a) for a in ("x", "z", "y", "c"))
    ix, iz, iy, ic = (lax.axis_index(a) for a in ("x", "z", "y", "c"))
    n_blk, n_head = nx * nz, ny * nc
    blk, head = ix * nz + iz, iy * nc + ic
    rows, width = acceptance_vector.shape
    embed = skip_stream_input.shape[1]
    pairs = width // LANES
    own = rows // n_head

    vocab_local = vocabulary_readout.shape[0]
    share = vocab_local // n_head
    own_columns = closing_projection.shape[1]
    fold = embed // width
    held = own_columns // fold
    early = share * 3 // 8
    block = closing_projection.T.reshape(fold, held, width).transpose(1, 0, 2).reshape(held, embed)
    rows_1 = jnp.concatenate(
        [block, lax.dynamic_slice_in_dim(vocabulary_readout, head * share, early)], axis=0
    )
    gathered_1 = lax.all_gather(rows_1, "z", axis=0, tiled=True)
    rows_2 = lax.dynamic_slice_in_dim(vocabulary_readout, head * share + early, share - early)
    rows_2, _ = lax.optimization_barrier((rows_2, rows_1))
    gathered_2 = lax.all_gather(rows_2, "z", axis=0, tiled=True)

    chunks = n_blk // pairs
    chunk_rows = CHAN // chunks
    col = pl.BlockSpec((rows, LANES), lambda p: (0, p))
    end = pl.pallas_call(
        functools.partial(block_end_kernel, chunk_rows),
        grid=(pairs,),
        in_specs=[col] * 3,
        out_specs=pl.BlockSpec((chunks, 2 * chunk_rows, LANES), lambda p: (p, 0, 0)),
        out_shape=jax.ShapeDtypeStruct((n_blk, 2 * chunk_rows, LANES), F32),
        cost_estimate=cost(pairs * 20_000_000, 3 * rows * width * 2),
    )(lookup_vector_array, payload_vector_array, raw_forgetting_rate)
    moved = lax.all_to_all(end, ("x", "z"), 0, 0, tiled=True)

    facts, bonus, _ = lax.optimization_barrier(
        (
            jnp.concatenate(
                [
                    following_labels.astype(F32),
                    response_indicator.astype(F32),
                    baseline_logarithmic_likelihood,
                ]
            ),
            current_reward_vector[None, :],
            end,
        )
    )
    plane = nx * ny * nc
    facts = jnp.pad(facts, (0, LANES - 3 * own)).reshape(1, LANES)
    facts = spread(facts, "c", [list(range(nc))])
    facts = spread(facts, "y", [list(range(ny))])
    row = pl.BlockSpec((1, LANES), lambda p: (0, p))
    within, high, low = pl.pallas_call(
        within_kernel,
        grid=(pairs,),
        in_specs=[col] * 4 + [row],
        out_specs=[col] * 3,
        out_shape=[jax.ShapeDtypeStruct((rows, width), t) for t in (F32, BF16, BF16)],
        cost_estimate=cost(pairs * 60_000_000, 8 * rows * width * 2),
    )(acceptance_vector, lookup_vector_array, payload_vector_array, raw_forgetting_rate, bonus)

    moved, within, high, low, facts = lax.optimization_barrier((moved, within, high, low, facts))
    prev_seq = jnp.concatenate([jnp.full((1,), -1, jnp.int32), rollout_for_segment[:-1]])
    starts = (rollout_for_segment != prev_seq).astype(jnp.int32)
    meta = jnp.stack([starts, query_text_for_rollout[rollout_for_segment]])
    prompts = memory_following_query.shape[0]
    prompt = lax.dynamic_slice(
        memory_following_query.reshape(prompts, pairs, 2, CHAN, CHAN),
        (0, blk // chunks, 0, (blk % chunks) * chunk_rows, 0),
        (prompts, 1, 2, chunk_rows, CHAN),
    )[:, 0]
    prompt = prompt.transpose(0, 2, 1, 3).reshape(prompts, chunk_rows, LANES).astype(F32)
    vmem = pl.BlockSpec(memory_space=pltpu.VMEM)
    entering = pl.pallas_call(
        functools.partial(relay_kernel, chunk_rows),
        in_specs=[pl.BlockSpec(memory_space=pltpu.SMEM), vmem, vmem],
        out_specs=vmem,
        out_shape=jax.ShapeDtypeStruct((n_blk, chunk_rows, LANES), F32),
        cost_estimate=cost(1_000_000, 500_000),
    )(meta, moved, prompt)
    entering = lax.all_to_all(entering, ("x", "z"), 0, 0, tiled=True)
    entering = entering.reshape(pairs * CHAN, LANES)

    mixed = pl.pallas_call(
        mix_kernel,
        grid=(pairs,),
        in_specs=[col] * 4 + [row, pl.BlockSpec((CHAN, LANES), lambda p: (p, 0))],
        out_specs=col,
        out_shape=jax.ShapeDtypeStruct((rows, width), BF16),
        cost_estimate=cost(pairs * 20_000_000, 6 * rows * width * 2),
    )(within, high, low, raw_gating_signal, group_layernorm_scaling[None, :], entering)

    columns = gathered_1.reshape(nz, held + early, embed)[:, :held]
    columns = jnp.concatenate(jnp.split(columns, fold, axis=2), axis=1)
    columns = columns.reshape(nz * own_columns, width)

    mixed = lax.all_gather(mixed, "x", axis=0)
    mixed = mixed.reshape(nx, ny, nc, own, width).transpose(2, 1, 0, 3, 4)
    mixed = mixed.reshape(nc, ny * nx * own, width)
    theirs = mm_t(lax.dynamic_index_in_dim(mixed, 1 - ic, 0, False), columns)
    mine = mm_t(lax.dynamic_index_in_dim(mixed, ic, 0, False), columns)
    partial = mine + shifted(theirs, "c", 1)
    partial = partial.reshape(ny * nx, own, embed // nx)
    partial, facts = lax.optimization_barrier((partial, facts))
    facts = spread(facts, "x", [list(range(nx))])
    partial = lax.all_to_all(partial, ("y", "x"), 0, 0, tiled=True)
    projected = jnp.sum(partial.reshape(ny, nx, own, embed // nx), axis=0)
    projected = projected.transpose(1, 0, 2).reshape(own, embed)
    hidden = skip_stream_input.astype(F32) + projected
    hmean = jnp.mean(hidden, axis=-1, keepdims=True)
    hvar = jnp.mean((hidden - hmean) ** 2, axis=-1, keepdims=True)
    normed = ((hidden - hmean) / jnp.sqrt(hvar + 1e-05) * closing_layernorm_scaling).astype(BF16)

    normed, facts = lax.optimization_barrier((normed, facts))
    facts = facts[..., 0, : 3 * own].reshape(nx, ny, nc, 3, own).transpose(3, 2, 1, 0, 4)

    tokens = copies(normed, ("y", "x")).reshape(ny * nx * own, embed)
    other = shifted(tokens, "c", 1)
    count = plane * own
    labels = facts[0].reshape(1, count).astype(jnp.int32)
    place = jnp.stack([ic, ix * nz * vocab_local + head * share]).astype(jnp.int32)

    def whole(*shape):
        return pl.BlockSpec(shape, lambda i: (0,) * len(shape))

    def score(vocab, layout, tile, known=None):
        first, height = known is None, 3 if known is None else 2
        return pl.pallas_call(
            functools.partial(score_kernel, layout, first, not first),
            grid=(vocab.shape[0] // tile,),
            in_specs=[
                pl.BlockSpec(memory_space=pltpu.SMEM),
                whole(count // nc, embed),
                whole(count // nc, embed),
                whole(1, count),
                pl.BlockSpec((tile, embed), lambda i: (i, 0)),
            ]
            + ([] if first else [whole(3, count)]),
            out_specs=whole(height, count),
            out_shape=jax.ShapeDtypeStruct((height, count), F32),
            scratch_shapes=[pltpu.VMEM((3, count), F32)],
            compiler_params=pltpu.CompilerParams(vmem_limit_bytes=56 * 1024 * 1024),
            cost_estimate=cost(
                2 * count * vocab.shape[0] * embed, (count + vocab.shape[0]) * embed * 2
            ),
        )(place, tokens, other, labels, vocab, *([] if first else [known]))

    known = score(gathered_1, (held + early, held, 0, vocab_local), gathered_1.shape[0])
    late = gathered_2.shape[0] // 2
    both = score(gathered_2, (share - early, 0, early, vocab_local), late, known)
    both = copies(both, ("x", "y", "c"))
    part, picked = both[:, 0], both[:, 1]
    peak = jnp.max(part, axis=0)
    logp = jnp.sum(picked, axis=0) - peak - jnp.log(jnp.sum(jnp.exp(part - peak), axis=0))
    ratio = facts[1] * (logp.reshape(nc, ny, nx, own) - facts[2])
    token_ratio = lax.dynamic_slice(ratio, (ic, iy, ix, 0), (1, 1, 1, own)).reshape(own)

    sums = jnp.sum(ratio, axis=(0, 1, 3))
    sums = copies(jnp.pad(sums, (0, LANES - nx)).reshape(1, LANES), "z")[:, 0, :nx]
    seq_of = rollout_for_segment.reshape(nx, nz).T
    marker = jnp.arange(query_text_for_rollout.shape[0])[:, None, None] == seq_of[None]
    seq_ratio = jnp.sum(jnp.where(marker, sums[None], 0.0), axis=(1, 2)) / TOK_BLK
    return (token_ratio, seq_ratio)


def solution(mesh):
    n_blk, n_head = mesh.devices.shape
    nx, nc = 4, 2
    fine = Mesh(
        mesh.devices.reshape(nx, n_blk // nx, n_head // nc, nc), ("x", "z", "y", "c")
    )
    blk, head = ("x", "z"), ("y", "c")
    placed = (
        P(blk, head),
        P(blk, head),
        P(blk, head),
        P(blk, head),
        P(blk, head),
        P(head),
        P(None, head, None),
        P(head),
        P(),
        P(blk + head, None),
        P(head, blk),
        P(blk, None),
        P(blk + head),
        P(blk + head),
        P(blk + head),
        P(),
        P(),
    )
    return jax.shard_map(
        per_device, mesh=fine, in_specs=placed, out_specs=(P(blk + head), P()), check_vma=False
    )
```

```python
import functools

import jax
import jax.numpy as jnp
from jax import lax
from jax.experimental import pallas as pl
from jax.experimental.pallas import tpu as pltpu
from jax.sharding import Mesh
from jax.sharding import PartitionSpec as P

CHAN = 64
LANES = 128
TOK_BLK = 128
SUB = 32
F32 = jnp.float32
BF16 = jnp.bfloat16


def parts2(a):
    high = a.astype(BF16)
    return high, (a - high.astype(F32)).astype(BF16)


def parts3(a):
    high, rest = a.astype(BF16), None
    rest = a - high.astype(F32)
    mid = rest.astype(BF16)
    return high, mid, (rest - mid.astype(F32)).astype(BF16)


def mm(a, b):
    return jnp.dot(a, b, preferred_element_type=F32)


def mm_t(a, b):
    return lax.dot_general(a, b, (((1,), (1,)), ((), ())), preferred_element_type=F32)


def running_log_decay(rate):
    log_decay = -jnp.exp(rate.astype(F32))
    rows = log_decay.shape[0]
    i = lax.broadcasted_iota(jnp.int32, (rows, rows), 0)
    j = lax.broadcasted_iota(jnp.int32, (rows, rows), 1)
    lower = (i >= j).astype(F32).astype(BF16)
    total = mm(
        jnp.concatenate([lower] * 3, axis=1), jnp.concatenate(parts3(log_decay), axis=0)
    )
    return log_decay, total


def left_lanes(rows):
    return lax.broadcasted_iota(jnp.int32, (rows, LANES), 1) < CHAN


def block_end_kernel(chunk_rows, k_ref, v_ref, w_ref, out_ref):
    _, inclusive = running_log_decay(w_ref[...])
    last = inclusive[TOK_BLK - 1 :, :]
    late = k_ref[...].astype(F32) * jnp.exp(last - inclusive)
    high, low = parts2(late.T)
    v = v_ref[...]
    both = mm(jnp.concatenate([high, low], axis=1), jnp.concatenate([v, v], axis=0))
    fall = jnp.exp(jnp.broadcast_to(last, (LANES, LANES)).T)
    left = left_lanes(CHAN)
    both = jnp.where(left, both[:CHAN], both[CHAN:])
    fall = jnp.where(left, fall[:CHAN], fall[CHAN:])
    for q in range(CHAN // chunk_rows):
        rows = slice(q * chunk_rows, (q + 1) * chunk_rows)
        out_ref[q, :chunk_rows, :] = both[rows]
        out_ref[q, chunk_rows:, :] = fall[rows]


def relay_kernel(chunk_rows, meta_ref, moved_ref, prompt_ref, out_ref):
    def step(b, state):
        prompt = jnp.where(meta_ref[1, b] == 0, prompt_ref[0], prompt_ref[1])
        state = jnp.where(meta_ref[0, b] != 0, prompt, state)
        out_ref[b] = state
        return moved_ref[b, chunk_rows:, :] * state + moved_ref[b, :chunk_rows, :]

    lax.fori_loop(
        0, moved_ref.shape[0], step, jnp.zeros((chunk_rows, LANES), F32), unroll=8
    )


def within_kernel(r_ref, k_ref, v_ref, w_ref, u_ref, wkv_ref, high_ref, low_ref):
    r = r_ref[...].astype(F32)
    k = k_ref[...].astype(F32)
    v = v_ref[...]
    log_decay, inclusive = running_log_decay(w_ref[...])
    exclusive = inclusive - log_decay
    left = left_lanes(SUB)
    pieces = []
    for sub in range(TOK_BLK // SUB):
        a, b = sub * SUB, (sub + 1) * SUB
        pivot = inclusive[a + SUB // 2 - 1 : a + SUB // 2, :]
        rs = r[a:b] * jnp.exp(exclusive[a:b] - pivot)
        ks = k[:b] * jnp.exp(pivot - inclusive[:b])
        rs = jnp.concatenate([jnp.where(left, rs, 0.0), jnp.where(left, 0.0, rs)], axis=0)
        rh, rl = parts2(rs)
        kh, kl = parts2(ks)
        scores = mm_t(
            jnp.concatenate([rh, rl, rh], axis=1), jnp.concatenate([kh, kh, kl], axis=1)
        )
        t = lax.broadcasted_iota(jnp.int32, scores.shape, 0) % SUB + a
        s = lax.broadcasted_iota(jnp.int32, scores.shape, 1)
        sh, sl = parts2(jnp.where(s < t, scores, 0.0))
        both = mm(sh, v[:b]) + mm(sl, v[:b])
        pieces.append(jnp.where(left, both[:SUB], both[SUB:]))
    now = mm(jnp.concatenate(parts2(r * k * u_ref[...]), axis=1), same_head(1.0))
    wkv_ref[...] = jnp.concatenate(pieces, axis=0) + now * v.astype(F32)
    high_ref[...], low_ref[...] = parts2(r * jnp.exp(exclusive))


def same_head(value):
    i = lax.broadcasted_iota(jnp.int32, (LANES, LANES), 0) // CHAN
    j = lax.broadcasted_iota(jnp.int32, (LANES, LANES), 1) // CHAN
    return jnp.concatenate([jnp.where(i == j, value, 0.0).astype(BF16)] * 2, axis=0)


def mix_kernel(wkv_ref, high_ref, low_ref, g_ref, scale_ref, state_ref, out_ref):
    state = state_ref[...]
    left = left_lanes(CHAN)
    state = jnp.concatenate([jnp.where(left, state, 0.0), jnp.where(left, 0.0, state)], axis=0)
    sh, sl = parts2(state)
    high = high_ref[...]
    wkv = wkv_ref[...] + mm(
        jnp.concatenate([high, low_ref[...], high], axis=1), jnp.concatenate([sh, sh, sl], axis=0)
    )
    mean_of = same_head(1.0 / CHAN)
    mean = mm(jnp.concatenate(parts2(wkv), axis=1), mean_of)
    off = wkv - mean
    var = mm(jnp.concatenate(parts2(off * off), axis=1), mean_of)
    g = g_ref[...].astype(F32)
    y = off / jnp.sqrt(var + 0.00064) * scale_ref[...]
    out_ref[...] = (y * (g / (1.0 + jnp.exp(-g)))).astype(out_ref.dtype)


def project_kernel(shape, place_ref, mixed_ref, block_ref, mine_ref, theirs_ref, columns_ref):
    ny, nc, own = shape
    fold, held = block_ref.shape[2] // columns_ref.shape[1], block_ref.shape[1]
    width = columns_ref.shape[1]
    for z in range(block_ref.shape[0]):
        for b in range(fold):
            at = (z * fold + b) * held
            columns_ref[at : at + held, :] = block_ref[z, :, b * width : (b + 1) * width]
    for out_ref, core in ((theirs_ref, 1 - place_ref[0]), (mine_ref, place_ref[0])):
        rows = [
            mixed_ref[x, pl.ds(pl.multiple_of((y * nc + core) * own, own), own), :]
            for y in range(ny)
            for x in range(mixed_ref.shape[0])
        ]
        out_ref[...] = mm_t(jnp.concatenate(rows, axis=0), columns_ref[...])


def score_kernel(
    layout, first, final, place_ref, mine_ref, theirs_ref, label_ref, vocab_ref, *refs
):
    group, skipped, offset, vocab_local = layout
    known_ref, (out_ref, state_ref) = (None, refs) if first else (refs[0], refs[1:])
    step = pl.program_id(0)
    tile, half = vocab_ref.shape[0], mine_ref.shape[0]
    core = place_ref[0]

    @pl.when(step == 0)
    def _():
        if first:
            state_ref[0:1] = jnp.full((1, 2 * half), -3.0e38, F32)
            state_ref[1:3] = jnp.zeros((2, 2 * half), F32)
        else:
            state_ref[...] = known_ref[...]

    index = step * tile + lax.broadcasted_iota(jnp.int32, (tile, 1), 0)
    source = lax.div(index, jnp.int32(group))
    row = index - source * group
    entry = jnp.where(
        row < skipped, -1, place_ref[1] + source * vocab_local + (row - skipped + offset)
    )
    for part, tokens in enumerate((mine_ref, theirs_ref)):
        at = slice(part * half, (part + 1) * half)
        label = jnp.where(core == part, label_ref[:, :half], label_ref[:, half:])
        logits = mm_t(vocab_ref[...], tokens[...])
        found = jnp.where(entry == label, logits, 0.0)
        if skipped:
            logits = jnp.where(entry < 0, -3.0e38, logits)
        old = state_ref[0:1, at]
        top = jnp.maximum(old, jnp.max(logits, axis=0, keepdims=True))
        fresh = jnp.sum(jnp.exp(logits - top), axis=0, keepdims=True)
        state_ref[1:2, at] = state_ref[1:2, at] * jnp.exp(old - top) + fresh
        state_ref[2:3, at] += jnp.sum(found, axis=0, keepdims=True)
        state_ref[0:1, at] = top

    @pl.when(step == pl.num_programs(0) - 1)
    def _():
        if not final:
            out_ref[...] = state_ref[...]
            return
        part = state_ref[0:1] + jnp.log(state_ref[1:2])
        for row, value in enumerate((part, state_ref[2:3])):
            left, right = value[:, :half], value[:, half:]
            out_ref[row : row + 1, :half] = jnp.where(core == 0, left, right)
            out_ref[row : row + 1, half:] = jnp.where(core == 0, right, left)


def cost(flops, nbytes):
    return pl.CostEstimate(flops=flops, bytes_accessed=nbytes, transcendentals=0)


def limit(mib):
    return pltpu.CompilerParams(vmem_limit_bytes=mib * 1024 * 1024)


def in_hbm(value):
    return pltpu.with_memory_space_constraint(value, pltpu.HBM)


def whole(*shape):
    return pl.BlockSpec(shape, lambda i: (0,) * len(shape))


def shifted(value, axis, steps):
    count = lax.axis_size(axis)
    return lax.ppermute(value, axis, [(i, (i + steps) % count) for i in range(count)])


def copies(value, axes):
    count = lax.axis_size(axes)
    sent = jnp.broadcast_to(value[None], (count, *value.shape))
    return lax.all_to_all(sent, axes, 0, 0, tiled=True)


def spread(value, axis, groups):
    count = len(groups[0])
    place = sum(
        jnp.where(lax.axis_index(axis) == source, i, 0)
        for group in groups
        for i, source in enumerate(group)
    )
    out = jnp.zeros((count, *value.shape), value.dtype)
    for step in range(count):
        pairs = [(g[i], g[(i + step) % count]) for g in groups for i in range(count)]
        piece = lax.ppermute(value, axis, pairs) if step else value
        out = lax.dynamic_update_index_in_dim(out, piece, (place - step) % count, 0)
    return out


def per_device(
    acceptance_vector,
    lookup_vector_array,
    payload_vector_array,
    raw_gating_signal,
    raw_forgetting_rate,
    current_reward_vector,
    memory_following_query,
    group_layernorm_scaling,
    closing_layernorm_scaling,
    skip_stream_input,
    closing_projection,
    vocabulary_readout,
    following_labels,
    response_indicator,
    baseline_logarithmic_likelihood,
    rollout_for_segment,
    query_text_for_rollout,
):
    nx, nz, ny, nc = (lax.axis_size(a) for a in ("x", "z", "y", "c"))
    ix, iz, iy, ic = (lax.axis_index(a) for a in ("x", "z", "y", "c"))
    n_blk, n_head = nx * nz, ny * nc
    blk, head = ix * nz + iz, iy * nc + ic
    rows, width = acceptance_vector.shape
    embed = skip_stream_input.shape[1]
    pairs = width // LANES
    own = rows // n_head

    vocab_local = vocabulary_readout.shape[0]
    share = vocab_local // n_head
    own_columns = closing_projection.shape[1]
    fold = embed // width
    held = own_columns // fold
    early = share // 4
    block = closing_projection.T.reshape(fold, held, width).transpose(1, 0, 2).reshape(held, embed)
    rows_1 = jnp.concatenate(
        [block, lax.dynamic_slice_in_dim(vocabulary_readout, head * share, early)], axis=0
    )
    gathered_1 = lax.all_gather(rows_1, "z", axis=0, tiled=True)

    chunks = n_blk // pairs
    chunk_rows = CHAN // chunks
    col = pl.BlockSpec((rows, LANES), lambda p: (0, p))
    end = pl.pallas_call(
        functools.partial(block_end_kernel, chunk_rows),
        grid=(pairs,),
        in_specs=[col] * 3,
        out_specs=pl.BlockSpec((chunks, 2 * chunk_rows, LANES), lambda p: (p, 0, 0)),
        out_shape=jax.ShapeDtypeStruct((n_blk, 2 * chunk_rows, LANES), F32),
        compiler_params=limit(60),
        cost_estimate=cost(pairs * 20_000_000, 3 * rows * width * 2),
    )(lookup_vector_array, payload_vector_array, raw_forgetting_rate)
    moved = lax.all_to_all(end, ("x", "z"), 0, 0, tiled=True)

    facts, bonus, _ = lax.optimization_barrier(
        (
            jnp.concatenate(
                [
                    following_labels.astype(F32),
                    response_indicator.astype(F32),
                    baseline_logarithmic_likelihood,
                ]
            ),
            current_reward_vector[None, :],
            end,
        )
    )
    plane = nx * ny * nc
    facts = jnp.pad(facts, (0, LANES - 3 * own)).reshape(1, LANES)
    facts = spread(facts, "c", [list(range(nc))])
    vocabulary, facts = lax.optimization_barrier((vocabulary_readout, facts))
    rows_2 = lax.dynamic_slice_in_dim(vocabulary, head * share + early, share - early)
    facts = spread(facts, "y", [list(range(ny))])
    row = pl.BlockSpec((1, LANES), lambda p: (0, p))
    within, high, low = pl.pallas_call(
        within_kernel,
        grid=(pairs,),
        in_specs=[col] * 4 + [row],
        out_specs=[col] * 3,
        out_shape=[jax.ShapeDtypeStruct((rows, width), t) for t in (F32, BF16, BF16)],
        compiler_params=limit(60),
        cost_estimate=cost(pairs * 60_000_000, 8 * rows * width * 2),
    )(acceptance_vector, lookup_vector_array, payload_vector_array, raw_forgetting_rate, bonus)

    prev_seq = jnp.concatenate([jnp.full((1,), -1, jnp.int32), rollout_for_segment[:-1]])
    starts = (rollout_for_segment != prev_seq).astype(jnp.int32)
    meta = jnp.stack([starts, query_text_for_rollout[rollout_for_segment]])
    prompts = memory_following_query.shape[0]
    prompt = lax.dynamic_slice(
        memory_following_query.reshape(prompts, pairs, 2, CHAN, CHAN),
        (0, blk // chunks, 0, (blk % chunks) * chunk_rows, 0),
        (prompts, 1, 2, chunk_rows, CHAN),
    )[:, 0]
    prompt = prompt.transpose(0, 2, 1, 3).reshape(prompts, chunk_rows, LANES).astype(F32)
    moved, within, high, low, facts, rows_2, meta, prompt = lax.optimization_barrier(
        (moved, within, high, low, facts, rows_2, meta, prompt)
    )
    gathered_2 = lax.all_gather(rows_2, "z", axis=0, tiled=True)
    vmem = pl.BlockSpec(memory_space=pltpu.VMEM)
    entering = pl.pallas_call(
        functools.partial(relay_kernel, chunk_rows),
        in_specs=[pl.BlockSpec(memory_space=pltpu.SMEM), vmem, vmem],
        out_specs=vmem,
        out_shape=jax.ShapeDtypeStruct((n_blk, chunk_rows, LANES), F32),
        compiler_params=limit(4),
        cost_estimate=cost(1_000_000, 500_000),
    )(meta, moved, prompt)
    entering = lax.all_to_all(entering, ("x", "z"), 0, 0, tiled=True)
    entering = entering.reshape(pairs * CHAN, LANES)

    mixed = pl.pallas_call(
        mix_kernel,
        grid=(pairs,),
        in_specs=[col] * 4 + [row, pl.BlockSpec((CHAN, LANES), lambda p: (p, 0))],
        out_specs=col,
        out_shape=jax.ShapeDtypeStruct((rows, width), BF16),
        compiler_params=limit(8),
        cost_estimate=cost(pairs * 20_000_000, 6 * rows * width * 2),
    )(within, high, low, raw_gating_signal, group_layernorm_scaling[None, :], entering)

    mixed = lax.all_gather(mixed, "x", axis=0)
    place = jnp.stack([ic, ix * nz * vocab_local + head * share]).astype(jnp.int32)
    half = jax.ShapeDtypeStruct((ny * nx * own, embed // nx), F32)
    smem = pl.BlockSpec(memory_space=pltpu.SMEM)
    mine, theirs = pl.pallas_call(
        functools.partial(project_kernel, (ny, nc, own)),
        grid=(1,),
        in_specs=[
            smem,
            whole(nx, rows, width),
            pl.BlockSpec((nz, held, embed), lambda i: (0, 0, 0)),
        ],
        out_specs=[whole(*half.shape)] * 2,
        out_shape=[half, half],
        scratch_shapes=[pltpu.VMEM((nz * own_columns, width), BF16)],
        compiler_params=limit(24),
        cost_estimate=cost(4 * half.size * width, 4_000_000),
    )(place, mixed, in_hbm(gathered_1.reshape(nz, held + early, embed)))
    partial = mine + shifted(theirs, "c", 1)
    partial = partial.reshape(ny * nx, own, embed // nx)
    partial, facts = lax.optimization_barrier((partial, facts))
    facts = spread(facts, "x", [list(range(nx))])
    partial = lax.all_to_all(partial, ("y", "x"), 0, 0, tiled=True)
    projected = jnp.sum(partial.reshape(ny, nx, own, embed // nx), axis=0)
    projected = projected.transpose(1, 0, 2).reshape(own, embed)
    hidden = skip_stream_input.astype(F32) + projected
    hmean = jnp.mean(hidden, axis=-1, keepdims=True)
    hvar = jnp.mean((hidden - hmean) ** 2, axis=-1, keepdims=True)
    normed = ((hidden - hmean) / jnp.sqrt(hvar + 1e-05) * closing_layernorm_scaling).astype(BF16)

    normed, facts = lax.optimization_barrier((normed, facts))

    tokens = copies(normed, ("y", "x")).reshape(ny * nx * own, embed)
    facts = facts[..., 0, : 3 * own].reshape(nx, ny, nc, 3, own).transpose(3, 2, 1, 0, 4)
    other = shifted(tokens, "c", 1)
    count = plane * own
    labels = facts[0].reshape(1, count).astype(jnp.int32)
    def score(vocab, layout, tile, known=None):
        first, height = known is None, 3 if known is None else 2
        return pl.pallas_call(
            functools.partial(score_kernel, layout, first, not first),
            grid=(vocab.shape[0] // tile,),
            in_specs=[
                smem,
                vmem,
                vmem,
                vmem,
                pl.BlockSpec((tile, embed), lambda i: (i, 0)),
            ]
            + ([] if first else [vmem]),
            out_specs=whole(height, count),
            out_shape=jax.ShapeDtypeStruct((height, count), F32),
            scratch_shapes=[pltpu.VMEM((3, count), F32)],
            compiler_params=limit(24),
            cost_estimate=cost(
                2 * count * vocab.shape[0] * embed, (count + vocab.shape[0]) * embed * 2
            ),
        )(place, tokens, other, labels, in_hbm(vocab), *([] if first else [known]))

    known = score(gathered_1, (held + early, held, 0, vocab_local), gathered_1.shape[0])
    late = gathered_2.shape[0] // 3
    both = score(gathered_2, (share - early, 0, early, vocab_local), late, known)
    both = copies(both, ("x", "y", "c"))
    part, picked = both[:, 0], both[:, 1]
    peak = jnp.max(part, axis=0)
    logp = jnp.sum(picked, axis=0) - peak - jnp.log(jnp.sum(jnp.exp(part - peak), axis=0))
    ratio = facts[1] * (logp.reshape(nc, ny, nx, own) - facts[2])
    token_ratio = lax.dynamic_slice(ratio, (ic, iy, ix, 0), (1, 1, 1, own)).reshape(own)

    sums = jnp.sum(ratio, axis=(0, 1, 3))
    sums = copies(jnp.pad(sums, (0, LANES - nx)).reshape(1, LANES), "z")[:, 0, :nx]
    seq_of = rollout_for_segment.reshape(nx, nz).T
    marker = jnp.arange(query_text_for_rollout.shape[0])[:, None, None] == seq_of[None]
    seq_ratio = jnp.sum(jnp.where(marker, sums[None], 0.0), axis=(1, 2)) / TOK_BLK
    return (token_ratio, seq_ratio)


def solution(mesh):
    n_blk, n_head = mesh.devices.shape
    nx, nc = 4, 2
    fine = Mesh(
        mesh.devices.reshape(nx, n_blk // nx, n_head // nc, nc), ("x", "z", "y", "c")
    )
    blk, head = ("x", "z"), ("y", "c")
    placed = (
        P(blk, head),
        P(blk, head),
        P(blk, head),
        P(blk, head),
        P(blk, head),
        P(head),
        P(None, head, None),
        P(head),
        P(),
        P(blk + head, None),
        P(head, blk),
        P(blk, None),
        P(blk + head),
        P(blk + head),
        P(blk + head),
        P(),
        P(),
    )
    return jax.shard_map(
        per_device, mesh=fine, in_specs=placed, out_specs=(P(blk + head), P()), check_vma=False
    )
```

```python
import functools

import jax
import jax.numpy as jnp
from jax import lax
from jax.experimental import pallas as pl
from jax.experimental.pallas import tpu as pltpu
from jax.sharding import Mesh
from jax.sharding import PartitionSpec as P

CHAN = 64
LANES = 128
TOK_BLK = 128
SUB = 32
F32 = jnp.float32
BF16 = jnp.bfloat16


def parts2(a):
    high = a.astype(BF16)
    return high, (a - high.astype(F32)).astype(BF16)


def parts3(a):
    high, rest = a.astype(BF16), None
    rest = a - high.astype(F32)
    mid = rest.astype(BF16)
    return high, mid, (rest - mid.astype(F32)).astype(BF16)


def mm(a, b):
    return jnp.dot(a, b, preferred_element_type=F32)


def mm_t(a, b):
    return lax.dot_general(a, b, (((1,), (1,)), ((), ())), preferred_element_type=F32)


def running_log_decay(rate):
    log_decay = -jnp.exp(rate.astype(F32))
    rows = log_decay.shape[0]
    i = lax.broadcasted_iota(jnp.int32, (rows, rows), 0)
    j = lax.broadcasted_iota(jnp.int32, (rows, rows), 1)
    lower = (i >= j).astype(F32).astype(BF16)
    total = mm(
        jnp.concatenate([lower] * 3, axis=1), jnp.concatenate(parts3(log_decay), axis=0)
    )
    return log_decay, total


def left_lanes(rows):
    return lax.broadcasted_iota(jnp.int32, (rows, LANES), 1) < CHAN


def block_end_kernel(chunk_rows, k_ref, v_ref, w_ref, out_ref):
    _, inclusive = running_log_decay(w_ref[...])
    last = inclusive[TOK_BLK - 1 :, :]
    late = k_ref[...].astype(F32) * jnp.exp(last - inclusive)
    high, low = parts2(late.T)
    v = v_ref[...]
    both = mm(jnp.concatenate([high, low], axis=1), jnp.concatenate([v, v], axis=0))
    fall = jnp.exp(jnp.broadcast_to(last, (LANES, LANES)).T)
    left = left_lanes(CHAN)
    both = jnp.where(left, both[:CHAN], both[CHAN:])
    fall = jnp.where(left, fall[:CHAN], fall[CHAN:])
    for q in range(CHAN // chunk_rows):
        rows = slice(q * chunk_rows, (q + 1) * chunk_rows)
        out_ref[q, :chunk_rows, :] = both[rows]
        out_ref[q, chunk_rows:, :] = fall[rows]


def relay_kernel(chunk_rows, meta_ref, moved_ref, prompt_ref, out_ref):
    def step(b, state):
        prompt = jnp.where(meta_ref[1, b] == 0, prompt_ref[0], prompt_ref[1])
        state = jnp.where(meta_ref[0, b] != 0, prompt, state)
        out_ref[b] = state
        return moved_ref[b, chunk_rows:, :] * state + moved_ref[b, :chunk_rows, :]

    lax.fori_loop(
        0, moved_ref.shape[0], step, jnp.zeros((chunk_rows, LANES), F32), unroll=8
    )


def within_kernel(r_ref, k_ref, v_ref, w_ref, u_ref, wkv_ref, high_ref, low_ref):
    r = r_ref[...].astype(F32)
    k = k_ref[...].astype(F32)
    v = v_ref[...]
    log_decay, inclusive = running_log_decay(w_ref[...])
    exclusive = inclusive - log_decay
    left = left_lanes(SUB)
    pieces = []
    for sub in range(TOK_BLK // SUB):
        a, b = sub * SUB, (sub + 1) * SUB
        pivot = inclusive[a + SUB // 2 - 1 : a + SUB // 2, :]
        rs = r[a:b] * jnp.exp(exclusive[a:b] - pivot)
        ks = k[:b] * jnp.exp(pivot - inclusive[:b])
        rs = jnp.concatenate([jnp.where(left, rs, 0.0), jnp.where(left, 0.0, rs)], axis=0)
        rh, rl = parts2(rs)
        kh, kl = parts2(ks)
        scores = mm_t(
            jnp.concatenate([rh, rl, rh], axis=1), jnp.concatenate([kh, kh, kl], axis=1)
        )
        t = lax.broadcasted_iota(jnp.int32, scores.shape, 0) % SUB + a
        s = lax.broadcasted_iota(jnp.int32, scores.shape, 1)
        sh, sl = parts2(jnp.where(s < t, scores, 0.0))
        both = mm(sh, v[:b]) + mm(sl, v[:b])
        pieces.append(jnp.where(left, both[:SUB], both[SUB:]))
    now = mm(jnp.concatenate(parts2(r * k * u_ref[...]), axis=1), same_head(1.0))
    wkv_ref[...] = jnp.concatenate(pieces, axis=0) + now * v.astype(F32)
    high_ref[...], low_ref[...] = parts2(r * jnp.exp(exclusive))


def same_head(value):
    i = lax.broadcasted_iota(jnp.int32, (LANES, LANES), 0) // CHAN
    j = lax.broadcasted_iota(jnp.int32, (LANES, LANES), 1) // CHAN
    return jnp.concatenate([jnp.where(i == j, value, 0.0).astype(BF16)] * 2, axis=0)


def mix_kernel(wkv_ref, high_ref, low_ref, g_ref, scale_ref, state_ref, out_ref):
    state = state_ref[...]
    left = left_lanes(CHAN)
    state = jnp.concatenate([jnp.where(left, state, 0.0), jnp.where(left, 0.0, state)], axis=0)
    sh, sl = parts2(state)
    high = high_ref[...]
    wkv = wkv_ref[...] + mm(
        jnp.concatenate([high, low_ref[...], high], axis=1), jnp.concatenate([sh, sh, sl], axis=0)
    )
    mean_of = same_head(1.0 / CHAN)
    mean = mm(jnp.concatenate(parts2(wkv), axis=1), mean_of)
    off = wkv - mean
    var = mm(jnp.concatenate(parts2(off * off), axis=1), mean_of)
    g = g_ref[...].astype(F32)
    y = off / jnp.sqrt(var + 0.00064) * scale_ref[...]
    out_ref[...] = (y * (g / (1.0 + jnp.exp(-g)))).astype(out_ref.dtype)


def project_kernel(shape, place_ref, mixed_ref, block_ref, mine_ref, theirs_ref, columns_ref):
    ny, nc, own = shape
    fold, held = block_ref.shape[2] // columns_ref.shape[1], block_ref.shape[1]
    width = columns_ref.shape[1]
    for z in range(block_ref.shape[0]):
        for b in range(fold):
            at = (z * fold + b) * held
            columns_ref[at : at + held, :] = block_ref[z, :, b * width : (b + 1) * width]
    for out_ref, core in ((theirs_ref, 1 - place_ref[0]), (mine_ref, place_ref[0])):
        rows = [
            mixed_ref[x, pl.ds(pl.multiple_of((y * nc + core) * own, own), own), :]
            for y in range(ny)
            for x in range(mixed_ref.shape[0])
        ]
        out_ref[...] = mm_t(jnp.concatenate(rows, axis=0), columns_ref[...])


def score_kernel(
    layout, first, final, place_ref, mine_ref, theirs_ref, label_ref, vocab_ref, *refs
):
    group, skipped, offset, vocab_local = layout
    known_ref, (out_ref, state_ref) = (None, refs) if first else (refs[0], refs[1:])
    step = pl.program_id(0)
    tile, half = vocab_ref.shape[0], mine_ref.shape[0]
    core = place_ref[0]

    @pl.when(step == 0)
    def _():
        if first:
            state_ref[0:1] = jnp.full((1, 2 * half), -3.0e38, F32)
            state_ref[1:3] = jnp.zeros((2, 2 * half), F32)
        else:
            state_ref[...] = known_ref[...]

    index = step * tile + lax.broadcasted_iota(jnp.int32, (tile, 1), 0)
    source = lax.div(index, jnp.int32(group))
    row = index - source * group
    entry = jnp.where(
        row < skipped, -1, place_ref[1] + source * vocab_local + (row - skipped + offset)
    )
    for part, tokens in enumerate((mine_ref, theirs_ref)):
        at = slice(part * half, (part + 1) * half)
        label = jnp.where(core == part, label_ref[:, :half], label_ref[:, half:])
        logits = mm_t(vocab_ref[...], tokens[...])
        found = jnp.where(entry == label, logits, 0.0)
        if skipped:
            logits = jnp.where(entry < 0, -3.0e38, logits)
        old = state_ref[0:1, at]
        top = jnp.maximum(old, jnp.max(logits, axis=0, keepdims=True))
        fresh = jnp.sum(jnp.exp(logits - top), axis=0, keepdims=True)
        state_ref[1:2, at] = state_ref[1:2, at] * jnp.exp(old - top) + fresh
        state_ref[2:3, at] += jnp.sum(found, axis=0, keepdims=True)
        state_ref[0:1, at] = top

    @pl.when(step == pl.num_programs(0) - 1)
    def _():
        if not final:
            out_ref[...] = state_ref[...]
            return
        part = state_ref[0:1] + jnp.log(state_ref[1:2])
        for row, value in enumerate((part, state_ref[2:3])):
            left, right = value[:, :half], value[:, half:]
            out_ref[row : row + 1, :half] = jnp.where(core == 0, left, right)
            out_ref[row : row + 1, half:] = jnp.where(core == 0, right, left)


def cost(flops, nbytes):
    return pl.CostEstimate(flops=flops, bytes_accessed=nbytes, transcendentals=0)


def limit(mib):
    return pltpu.CompilerParams(vmem_limit_bytes=mib * 1024 * 1024)


def in_hbm(value):
    return pltpu.with_memory_space_constraint(value, pltpu.HBM)


def whole(*shape):
    return pl.BlockSpec(shape, lambda i: (0,) * len(shape))


def shifted(value, axis, steps):
    count = lax.axis_size(axis)
    return lax.ppermute(value, axis, [(i, (i + steps) % count) for i in range(count)])


def copies(value, axes):
    count = lax.axis_size(axes)
    sent = jnp.broadcast_to(value[None], (count, *value.shape))
    return lax.all_to_all(sent, axes, 0, 0, tiled=True)


def spread(value, axis, groups):
    count = len(groups[0])
    place = sum(
        jnp.where(lax.axis_index(axis) == source, i, 0)
        for group in groups
        for i, source in enumerate(group)
    )
    out = jnp.zeros((count, *value.shape), value.dtype)
    for step in range(count):
        pairs = [(g[i], g[(i + step) % count]) for g in groups for i in range(count)]
        piece = lax.ppermute(value, axis, pairs) if step else value
        out = lax.dynamic_update_index_in_dim(out, piece, (place - step) % count, 0)
    return out


def per_device(
    acceptance_vector,
    lookup_vector_array,
    payload_vector_array,
    raw_gating_signal,
    raw_forgetting_rate,
    current_reward_vector,
    memory_following_query,
    group_layernorm_scaling,
    closing_layernorm_scaling,
    skip_stream_input,
    closing_projection,
    vocabulary_readout,
    following_labels,
    response_indicator,
    baseline_logarithmic_likelihood,
    rollout_for_segment,
    query_text_for_rollout,
):
    nx, nz, ny, nc = (lax.axis_size(a) for a in ("x", "z", "y", "c"))
    ix, iz, iy, ic = (lax.axis_index(a) for a in ("x", "z", "y", "c"))
    n_blk, n_head = nx * nz, ny * nc
    blk, head = ix * nz + iz, iy * nc + ic
    rows, width = acceptance_vector.shape
    embed = skip_stream_input.shape[1]
    pairs = width // LANES
    own = rows // n_head

    vocab_local = vocabulary_readout.shape[0]
    share = vocab_local // n_head
    own_columns = closing_projection.shape[1]
    fold = embed // width
    held = own_columns // fold
    early = share * 3 // 8
    block = closing_projection.T.reshape(fold, held, width).transpose(1, 0, 2).reshape(held, embed)
    rows_1 = jnp.concatenate(
        [block, lax.dynamic_slice_in_dim(vocabulary_readout, head * share, early)], axis=0
    )
    gathered_1 = lax.all_gather(rows_1, "z", axis=0, tiled=True)

    chunks = n_blk // pairs
    chunk_rows = CHAN // chunks
    col = pl.BlockSpec((rows, LANES), lambda p: (0, p))
    end = pl.pallas_call(
        functools.partial(block_end_kernel, chunk_rows),
        grid=(pairs,),
        in_specs=[col] * 3,
        out_specs=pl.BlockSpec((chunks, 2 * chunk_rows, LANES), lambda p: (p, 0, 0)),
        out_shape=jax.ShapeDtypeStruct((n_blk, 2 * chunk_rows, LANES), F32),
        compiler_params=limit(60),
        cost_estimate=cost(pairs * 20_000_000, 3 * rows * width * 2),
    )(lookup_vector_array, payload_vector_array, raw_forgetting_rate)
    moved = lax.all_to_all(end, ("x", "z"), 0, 0, tiled=True)

    facts, bonus, _ = lax.optimization_barrier(
        (
            jnp.concatenate(
                [
                    following_labels.astype(F32),
                    response_indicator.astype(F32),
                    baseline_logarithmic_likelihood,
                ]
            ),
            current_reward_vector[None, :],
            end,
        )
    )
    plane = nx * ny * nc
    facts = jnp.pad(facts, (0, LANES - 3 * own)).reshape(1, LANES)
    row = pl.BlockSpec((1, LANES), lambda p: (0, p))
    within, high, low = pl.pallas_call(
        within_kernel,
        grid=(pairs,),
        in_specs=[col] * 4 + [row],
        out_specs=[col] * 3,
        out_shape=[jax.ShapeDtypeStruct((rows, width), t) for t in (F32, BF16, BF16)],
        compiler_params=limit(60),
        cost_estimate=cost(pairs * 60_000_000, 8 * rows * width * 2),
    )(acceptance_vector, lookup_vector_array, payload_vector_array, raw_forgetting_rate, bonus)

    prev_seq = jnp.concatenate([jnp.full((1,), -1, jnp.int32), rollout_for_segment[:-1]])
    starts = (rollout_for_segment != prev_seq).astype(jnp.int32)
    meta = jnp.stack([starts, query_text_for_rollout[rollout_for_segment]])
    prompts = memory_following_query.shape[0]
    prompt = lax.dynamic_slice(
        memory_following_query.reshape(prompts, pairs, 2, CHAN, CHAN),
        (0, blk // chunks, 0, (blk % chunks) * chunk_rows, 0),
        (prompts, 1, 2, chunk_rows, CHAN),
    )[:, 0]
    prompt = prompt.transpose(0, 2, 1, 3).reshape(prompts, chunk_rows, LANES).astype(F32)
    vocabulary, within = lax.optimization_barrier((vocabulary_readout, within))
    rows_2 = lax.dynamic_slice_in_dim(vocabulary, head * share + early, share - early)
    moved, within, high, low, facts, rows_2, meta, prompt = lax.optimization_barrier(
        (moved, within, high, low, facts, rows_2, meta, prompt)
    )
    gathered_2 = lax.all_gather(rows_2, "z", axis=0, tiled=True)
    vmem = pl.BlockSpec(memory_space=pltpu.VMEM)
    entering = pl.pallas_call(
        functools.partial(relay_kernel, chunk_rows),
        in_specs=[pl.BlockSpec(memory_space=pltpu.SMEM), vmem, vmem],
        out_specs=vmem,
        out_shape=jax.ShapeDtypeStruct((n_blk, chunk_rows, LANES), F32),
        compiler_params=limit(4),
        cost_estimate=cost(1_000_000, 500_000),
    )(meta, moved, prompt)
    facts, _ = lax.optimization_barrier((facts, entering))
    entering = lax.all_to_all(entering, ("x", "z"), 0, 0, tiled=True)
    facts = spread(facts, "c", [list(range(nc))])
    facts = spread(facts, "y", [list(range(ny))])
    entering, facts = lax.optimization_barrier((entering, facts))
    entering = entering.reshape(pairs * CHAN, LANES)

    mixed = pl.pallas_call(
        mix_kernel,
        grid=(pairs,),
        in_specs=[col] * 4 + [row, pl.BlockSpec((CHAN, LANES), lambda p: (p, 0))],
        out_specs=col,
        out_shape=jax.ShapeDtypeStruct((rows, width), BF16),
        compiler_params=limit(8),
        cost_estimate=cost(pairs * 20_000_000, 6 * rows * width * 2),
    )(within, high, low, raw_gating_signal, group_layernorm_scaling[None, :], entering)

    mixed = lax.all_gather(mixed, "x", axis=0)
    place = jnp.stack([ic, ix * nz * vocab_local + head * share]).astype(jnp.int32)
    half = jax.ShapeDtypeStruct((ny * nx * own, embed // nx), F32)
    smem = pl.BlockSpec(memory_space=pltpu.SMEM)
    mine, theirs = pl.pallas_call(
        functools.partial(project_kernel, (ny, nc, own)),
        grid=(1,),
        in_specs=[
            smem,
            whole(nx, rows, width),
            pl.BlockSpec((nz, held, embed), lambda i: (0, 0, 0)),
        ],
        out_specs=[whole(*half.shape)] * 2,
        out_shape=[half, half],
        scratch_shapes=[pltpu.VMEM((nz * own_columns, width), BF16)],
        compiler_params=limit(24),
        cost_estimate=cost(4 * half.size * width, 4_000_000),
    )(place, mixed, in_hbm(gathered_1.reshape(nz, held + early, embed)))
    partial = mine + shifted(theirs, "c", 1)
    partial = partial.reshape(ny * nx, own, embed // nx)
    partial, facts = lax.optimization_barrier((partial, facts))
    facts = spread(facts, "x", [list(range(nx))])
    partial = lax.all_to_all(partial, ("y", "x"), 0, 0, tiled=True)
    projected = jnp.sum(partial.reshape(ny, nx, own, embed // nx), axis=0)
    projected = projected.transpose(1, 0, 2).reshape(own, embed)
    hidden = skip_stream_input.astype(F32) + projected
    hmean = jnp.mean(hidden, axis=-1, keepdims=True)
    hvar = jnp.mean((hidden - hmean) ** 2, axis=-1, keepdims=True)
    normed = ((hidden - hmean) / jnp.sqrt(hvar + 1e-05) * closing_layernorm_scaling).astype(BF16)

    normed, facts = lax.optimization_barrier((normed, facts))

    tokens = copies(normed, ("y", "x")).reshape(ny * nx * own, embed)
    facts = facts[..., 0, : 3 * own].reshape(nx, ny, nc, 3, own).transpose(3, 2, 1, 0, 4)
    other = shifted(tokens, "c", 1)
    count = plane * own
    labels = facts[0].reshape(1, count).astype(jnp.int32)
    def score(vocab, layout, tile, known=None):
        first, height = known is None, 3 if known is None else 2
        return pl.pallas_call(
            functools.partial(score_kernel, layout, first, not first),
            grid=(vocab.shape[0] // tile,),
            in_specs=[
                smem,
                vmem,
                vmem,
                vmem,
                pl.BlockSpec((tile, embed), lambda i: (i, 0)),
            ]
            + ([] if first else [vmem]),
            out_specs=whole(height, count),
            out_shape=jax.ShapeDtypeStruct((height, count), F32),
            scratch_shapes=[pltpu.VMEM((3, count), F32)],
            compiler_params=limit(24),
            cost_estimate=cost(
                2 * count * vocab.shape[0] * embed, (count + vocab.shape[0]) * embed * 2
            ),
        )(place, tokens, other, labels, in_hbm(vocab), *([] if first else [known]))

    known = score(gathered_1, (held + early, held, 0, vocab_local), gathered_1.shape[0])
    late = gathered_2.shape[0] // 2
    both = score(gathered_2, (share - early, 0, early, vocab_local), late, known)
    both = copies(both, ("x", "y", "c"))
    part, picked = both[:, 0], both[:, 1]
    peak = jnp.max(part, axis=0)
    logp = jnp.sum(picked, axis=0) - peak - jnp.log(jnp.sum(jnp.exp(part - peak), axis=0))
    ratio = facts[1] * (logp.reshape(nc, ny, nx, own) - facts[2])
    token_ratio = lax.dynamic_slice(ratio, (ic, iy, ix, 0), (1, 1, 1, own)).reshape(own)

    sums = jnp.sum(ratio, axis=(0, 1, 3))
    sums = copies(jnp.pad(sums, (0, LANES - nx)).reshape(1, LANES), "z")[:, 0, :nx]
    seq_of = rollout_for_segment.reshape(nx, nz).T
    marker = jnp.arange(query_text_for_rollout.shape[0])[:, None, None] == seq_of[None]
    seq_ratio = jnp.sum(jnp.where(marker, sums[None], 0.0), axis=(1, 2)) / TOK_BLK
    return (token_ratio, seq_ratio)


def solution(mesh):
    n_blk, n_head = mesh.devices.shape
    nx, nc = 4, 2
    fine = Mesh(
        mesh.devices.reshape(nx, n_blk // nx, n_head // nc, nc), ("x", "z", "y", "c")
    )
    blk, head = ("x", "z"), ("y", "c")
    placed = (
        P(blk, head),
        P(blk, head),
        P(blk, head),
        P(blk, head),
        P(blk, head),
        P(head),
        P(None, head, None),
        P(head),
        P(),
        P(blk + head, None),
        P(head, blk),
        P(blk, None),
        P(blk + head),
        P(blk + head),
        P(blk + head),
        P(),
        P(),
    )
    return jax.shard_map(
        per_device, mesh=fine, in_specs=placed, out_specs=(P(blk + head), P()), check_vma=False
    )
```

```python
import functools

import jax
import jax.numpy as jnp
from jax import lax
from jax.experimental import pallas as pl
from jax.experimental.pallas import tpu as pltpu
from jax.sharding import Mesh
from jax.sharding import PartitionSpec as P

CHAN = 64
LANES = 128
TOK_BLK = 128
SUB = 32
F32 = jnp.float32
BF16 = jnp.bfloat16


def parts2(a):
    high = a.astype(BF16)
    return high, (a - high.astype(F32)).astype(BF16)


def parts3(a):
    high, rest = a.astype(BF16), None
    rest = a - high.astype(F32)
    mid = rest.astype(BF16)
    return high, mid, (rest - mid.astype(F32)).astype(BF16)


def mm(a, b):
    return jnp.dot(a, b, preferred_element_type=F32)


def mm_t(a, b):
    return lax.dot_general(a, b, (((1,), (1,)), ((), ())), preferred_element_type=F32)


def running_log_decay(rate):
    log_decay = -jnp.exp(rate.astype(F32))
    rows = log_decay.shape[0]
    i = lax.broadcasted_iota(jnp.int32, (rows, rows), 0)
    j = lax.broadcasted_iota(jnp.int32, (rows, rows), 1)
    lower = (i >= j).astype(F32).astype(BF16)
    total = mm(
        jnp.concatenate([lower] * 3, axis=1), jnp.concatenate(parts3(log_decay), axis=0)
    )
    return log_decay, total


def left_lanes(rows):
    return lax.broadcasted_iota(jnp.int32, (rows, LANES), 1) < CHAN


def block_end_kernel(chunk_rows, k_ref, v_ref, w_ref, out_ref):
    _, inclusive = running_log_decay(w_ref[...])
    last = inclusive[TOK_BLK - 1 :, :]
    late = k_ref[...].astype(F32) * jnp.exp(last - inclusive)
    high, low = parts2(late.T)
    v = v_ref[...]
    both = mm(jnp.concatenate([high, low], axis=1), jnp.concatenate([v, v], axis=0))
    fall = jnp.exp(jnp.broadcast_to(last, (LANES, LANES)).T)
    left = left_lanes(CHAN)
    both = jnp.where(left, both[:CHAN], both[CHAN:])
    fall = jnp.where(left, fall[:CHAN], fall[CHAN:])
    span = CHAN // chunk_rows
    row = lax.broadcasted_iota(jnp.int32, (CHAN, LANES), 0) % chunk_rows
    lane = lax.broadcasted_iota(jnp.int32, (CHAN, LANES), 1) % CHAN // span
    fall = jnp.where(row == lane, fall, 0.0)
    for q in range(span):
        for r in range(chunk_rows):
            at = q * chunk_rows + r
            out_ref[q, :, r * LANES : (r + 1) * LANES] = both[at : at + 1]
        rows = slice(q * chunk_rows, (q + 1) * chunk_rows)
        out_ref[q, :, chunk_rows * LANES :] = jnp.sum(fall[rows], axis=0, keepdims=True)


def relay_kernel(chunk_rows, meta_ref, moved_ref, prompt_ref, out_ref):
    left = left_lanes(chunk_rows)
    row = lax.broadcasted_iota(jnp.int32, (chunk_rows, LANES), 0)
    lane = lax.broadcasted_iota(jnp.int32, (chunk_rows, LANES), 1) % CHAN
    chosen = lane == row * (CHAN // chunk_rows)

    def step(b, state):
        prompt = jnp.where(meta_ref[1, b] == 0, prompt_ref[0], prompt_ref[1])
        state = jnp.where(meta_ref[0, b] != 0, prompt, state)
        out_ref[b] = state
        change = jnp.concatenate(
            [moved_ref[b, :, r * LANES : (r + 1) * LANES] for r in range(chunk_rows)], axis=0
        )
        fall = moved_ref[b, :, chunk_rows * LANES :]
        fall = jnp.where(chosen, jnp.broadcast_to(fall, (chunk_rows, LANES)), 0.0)
        first = jnp.sum(jnp.where(left, fall, 0.0), axis=1, keepdims=True)
        second = jnp.sum(jnp.where(left, 0.0, fall), axis=1, keepdims=True)
        return jnp.where(left, first, second) * state + change

    lax.fori_loop(
        0, moved_ref.shape[0], step, jnp.zeros((chunk_rows, LANES), F32), unroll=8
    )


def within_kernel(r_ref, k_ref, v_ref, w_ref, u_ref, wkv_ref, high_ref, low_ref):
    r = r_ref[...].astype(F32)
    k = k_ref[...].astype(F32)
    v = v_ref[...]
    log_decay, inclusive = running_log_decay(w_ref[...])
    exclusive = inclusive - log_decay
    left = left_lanes(SUB)
    pieces = []
    for sub in range(TOK_BLK // SUB):
        a, b = sub * SUB, (sub + 1) * SUB
        pivot = inclusive[a + SUB // 2 - 1 : a + SUB // 2, :]
        rs = r[a:b] * jnp.exp(exclusive[a:b] - pivot)
        ks = k[:b] * jnp.exp(pivot - inclusive[:b])
        rs = jnp.concatenate([jnp.where(left, rs, 0.0), jnp.where(left, 0.0, rs)], axis=0)
        rh, rl = parts2(rs)
        kh, kl = parts2(ks)
        scores = mm_t(
            jnp.concatenate([rh, rl, rh], axis=1), jnp.concatenate([kh, kh, kl], axis=1)
        )
        t = lax.broadcasted_iota(jnp.int32, scores.shape, 0) % SUB + a
        s = lax.broadcasted_iota(jnp.int32, scores.shape, 1)
        sh, sl = parts2(jnp.where(s < t, scores, 0.0))
        both = mm(sh, v[:b]) + mm(sl, v[:b])
        pieces.append(jnp.where(left, both[:SUB], both[SUB:]))
    now = mm(jnp.concatenate(parts2(r * k * u_ref[...]), axis=1), same_head(1.0))
    wkv_ref[...] = jnp.concatenate(pieces, axis=0) + now * v.astype(F32)
    high_ref[...], low_ref[...] = parts2(r * jnp.exp(exclusive))


def same_head(value):
    i = lax.broadcasted_iota(jnp.int32, (LANES, LANES), 0) // CHAN
    j = lax.broadcasted_iota(jnp.int32, (LANES, LANES), 1) // CHAN
    return jnp.concatenate([jnp.where(i == j, value, 0.0).astype(BF16)] * 2, axis=0)


def mix_kernel(wkv_ref, high_ref, low_ref, g_ref, scale_ref, state_ref, out_ref):
    state = state_ref[...]
    left = left_lanes(CHAN)
    state = jnp.concatenate([jnp.where(left, state, 0.0), jnp.where(left, 0.0, state)], axis=0)
    sh, sl = parts2(state)
    high = high_ref[...]
    wkv = wkv_ref[...] + mm(
        jnp.concatenate([high, low_ref[...], high], axis=1), jnp.concatenate([sh, sh, sl], axis=0)
    )
    mean_of = same_head(1.0 / CHAN)
    mean = mm(jnp.concatenate(parts2(wkv), axis=1), mean_of)
    off = wkv - mean
    var = mm(jnp.concatenate(parts2(off * off), axis=1), mean_of)
    g = g_ref[...].astype(F32)
    y = off / jnp.sqrt(var + 0.00064) * scale_ref[...]
    out_ref[...] = (y * (g / (1.0 + jnp.exp(-g)))).astype(out_ref.dtype)


def project_kernel(shape, place_ref, mixed_ref, block_ref, mine_ref, theirs_ref, columns_ref):
    ny, nc, own = shape
    fold, held = block_ref.shape[2] // columns_ref.shape[1], block_ref.shape[1]
    width = columns_ref.shape[1]
    for z in range(block_ref.shape[0]):
        for b in range(fold):
            at = (z * fold + b) * held
            columns_ref[at : at + held, :] = block_ref[z, :, b * width : (b + 1) * width]
    for out_ref, core in ((theirs_ref, 1 - place_ref[0]), (mine_ref, place_ref[0])):
        rows = [
            mixed_ref[x, pl.ds(pl.multiple_of((y * nc + core) * own, own), own), :]
            for y in range(ny)
            for x in range(mixed_ref.shape[0])
        ]
        out_ref[...] = mm_t(jnp.concatenate(rows, axis=0), columns_ref[...])


def score_kernel(
    layout, first, final, place_ref, mine_ref, theirs_ref, label_ref, vocab_ref, *refs
):
    group, skipped, offset, vocab_local = layout
    known_ref, (out_ref, state_ref) = (None, refs) if first else (refs[0], refs[1:])
    step = pl.program_id(0)
    tile, half = vocab_ref.shape[0], mine_ref.shape[0]
    core = place_ref[0]

    @pl.when(step == 0)
    def _():
        if first:
            state_ref[0:1] = jnp.full((1, 2 * half), -3.0e38, F32)
            state_ref[1:3] = jnp.zeros((2, 2 * half), F32)
        else:
            state_ref[...] = known_ref[...]

    index = step * tile + lax.broadcasted_iota(jnp.int32, (tile, 1), 0)
    source = lax.div(index, jnp.int32(group))
    row = index - source * group
    entry = jnp.where(
        row < skipped, -1, place_ref[1] + source * vocab_local + (row - skipped + offset)
    )
    for part, tokens in enumerate((mine_ref, theirs_ref)):
        at = slice(part * half, (part + 1) * half)
        label = jnp.where(core == part, label_ref[:, :half], label_ref[:, half:])
        logits = mm_t(vocab_ref[...], tokens[...])
        found = jnp.where(entry == label, logits, 0.0)
        if skipped:
            logits = jnp.where(entry < 0, -3.0e38, logits)
        old = state_ref[0:1, at]
        top = jnp.maximum(old, jnp.max(logits, axis=0, keepdims=True))
        fresh = jnp.sum(jnp.exp(logits - top), axis=0, keepdims=True)
        state_ref[1:2, at] = state_ref[1:2, at] * jnp.exp(old - top) + fresh
        state_ref[2:3, at] += jnp.sum(found, axis=0, keepdims=True)
        state_ref[0:1, at] = top

    @pl.when(step == pl.num_programs(0) - 1)
    def _():
        if not final:
            out_ref[...] = state_ref[...]
            return
        part = state_ref[0:1] + jnp.log(state_ref[1:2])
        for row, value in enumerate((part, state_ref[2:3])):
            left, right = value[:, :half], value[:, half:]
            out_ref[row : row + 1, :half] = jnp.where(core == 0, left, right)
            out_ref[row : row + 1, half:] = jnp.where(core == 0, right, left)


def cost(flops, nbytes):
    return pl.CostEstimate(flops=flops, bytes_accessed=nbytes, transcendentals=0)


def limit(mib):
    return pltpu.CompilerParams(vmem_limit_bytes=mib * 1024 * 1024)


def in_hbm(value):
    return pltpu.with_memory_space_constraint(value, pltpu.HBM)


def whole(*shape):
    return pl.BlockSpec(shape, lambda i: (0,) * len(shape))


def shifted(value, axis, steps):
    count = lax.axis_size(axis)
    return lax.ppermute(value, axis, [(i, (i + steps) % count) for i in range(count)])


def copies(value, axes):
    count = lax.axis_size(axes)
    sent = jnp.broadcast_to(value[None], (count, *value.shape))
    return lax.all_to_all(sent, axes, 0, 0, tiled=True)


def spread(value, axis, groups):
    count = len(groups[0])
    place = sum(
        jnp.where(lax.axis_index(axis) == source, i, 0)
        for group in groups
        for i, source in enumerate(group)
    )
    out = jnp.zeros((count, *value.shape), value.dtype)
    for step in range(count):
        pairs = [(g[i], g[(i + step) % count]) for g in groups for i in range(count)]
        piece = lax.ppermute(value, axis, pairs) if step else value
        out = lax.dynamic_update_index_in_dim(out, piece, (place - step) % count, 0)
    return out


def per_device(
    acceptance_vector,
    lookup_vector_array,
    payload_vector_array,
    raw_gating_signal,
    raw_forgetting_rate,
    current_reward_vector,
    memory_following_query,
    group_layernorm_scaling,
    closing_layernorm_scaling,
    skip_stream_input,
    closing_projection,
    vocabulary_readout,
    following_labels,
    response_indicator,
    baseline_logarithmic_likelihood,
    rollout_for_segment,
    query_text_for_rollout,
):
    nx, nz, ny, nc = (lax.axis_size(a) for a in ("x", "z", "y", "c"))
    ix, iz, iy, ic = (lax.axis_index(a) for a in ("x", "z", "y", "c"))
    n_blk, n_head = nx * nz, ny * nc
    blk, head = ix * nz + iz, iy * nc + ic
    rows, width = acceptance_vector.shape
    embed = skip_stream_input.shape[1]
    pairs = width // LANES
    own = rows // n_head

    vocab_local = vocabulary_readout.shape[0]
    share = vocab_local // n_head
    own_columns = closing_projection.shape[1]
    fold = embed // width
    held = own_columns // fold
    early = share * 3 // 8
    block = closing_projection.T.reshape(fold, held, width).transpose(1, 0, 2).reshape(held, embed)
    rows_1 = jnp.concatenate(
        [block, lax.dynamic_slice_in_dim(vocabulary_readout, head * share, early)], axis=0
    )
    gathered_1 = lax.all_gather(rows_1, "z", axis=0, tiled=True)

    chunks = n_blk // pairs
    chunk_rows = CHAN // chunks
    col = pl.BlockSpec((rows, LANES), lambda p: (0, p))
    end = pl.pallas_call(
        functools.partial(block_end_kernel, chunk_rows),
        grid=(pairs,),
        in_specs=[col] * 3,
        out_specs=pl.BlockSpec((chunks, 1, (chunk_rows + 1) * LANES), lambda p: (p, 0, 0)),
        out_shape=jax.ShapeDtypeStruct((n_blk, 1, (chunk_rows + 1) * LANES), F32),
        compiler_params=limit(60),
        cost_estimate=cost(pairs * 20_000_000, 3 * rows * width * 2),
    )(lookup_vector_array, payload_vector_array, raw_forgetting_rate)
    moved = lax.all_to_all(end, ("x", "z"), 0, 0, tiled=True)

    facts, bonus, _ = lax.optimization_barrier(
        (
            jnp.concatenate(
                [
                    following_labels.astype(F32),
                    response_indicator.astype(F32),
                    baseline_logarithmic_likelihood,
                ]
            ),
            current_reward_vector[None, :],
            end,
        )
    )
    plane = nx * ny * nc
    facts = jnp.pad(facts, (0, LANES - 3 * own)).reshape(1, LANES)
    row = pl.BlockSpec((1, LANES), lambda p: (0, p))
    within, high, low = pl.pallas_call(
        within_kernel,
        grid=(pairs,),
        in_specs=[col] * 4 + [row],
        out_specs=[col] * 3,
        out_shape=[jax.ShapeDtypeStruct((rows, width), t) for t in (F32, BF16, BF16)],
        compiler_params=limit(60),
        cost_estimate=cost(pairs * 60_000_000, 8 * rows * width * 2),
    )(acceptance_vector, lookup_vector_array, payload_vector_array, raw_forgetting_rate, bonus)

    prev_seq = jnp.concatenate([jnp.full((1,), -1, jnp.int32), rollout_for_segment[:-1]])
    starts = (rollout_for_segment != prev_seq).astype(jnp.int32)
    meta = jnp.stack([starts, query_text_for_rollout[rollout_for_segment]])
    prompts = memory_following_query.shape[0]
    prompt = lax.dynamic_slice(
        memory_following_query.reshape(prompts, pairs, 2, CHAN, CHAN),
        (0, blk // chunks, 0, (blk % chunks) * chunk_rows, 0),
        (prompts, 1, 2, chunk_rows, CHAN),
    )[:, 0]
    prompt = prompt.transpose(0, 2, 1, 3).reshape(prompts, chunk_rows, LANES).astype(F32)
    vocabulary, within = lax.optimization_barrier((vocabulary_readout, within))
    rows_2 = lax.dynamic_slice_in_dim(vocabulary, head * share + early, share - early)
    moved, within, high, low, facts, rows_2, meta, prompt = lax.optimization_barrier(
        (moved, within, high, low, facts, rows_2, meta, prompt)
    )
    gathered_2 = lax.all_gather(rows_2, "z", axis=0, tiled=True)
    vmem = pl.BlockSpec(memory_space=pltpu.VMEM)
    entering = pl.pallas_call(
        functools.partial(relay_kernel, chunk_rows),
        in_specs=[pl.BlockSpec(memory_space=pltpu.SMEM), vmem, vmem],
        out_specs=vmem,
        out_shape=jax.ShapeDtypeStruct((n_blk, chunk_rows, LANES), F32),
        compiler_params=limit(4),
        cost_estimate=cost(1_000_000, 500_000),
    )(meta, moved, prompt)
    facts, _ = lax.optimization_barrier((facts, entering))
    entering = lax.all_to_all(entering, ("x", "z"), 0, 0, tiled=True)
    facts = spread(facts, "c", [list(range(nc))])
    facts = spread(facts, "y", [list(range(ny))])
    entering, facts = lax.optimization_barrier((entering, facts))
    entering = entering.reshape(pairs * CHAN, LANES)

    mixed = pl.pallas_call(
        mix_kernel,
        grid=(pairs,),
        in_specs=[col] * 4 + [row, pl.BlockSpec((CHAN, LANES), lambda p: (p, 0))],
        out_specs=col,
        out_shape=jax.ShapeDtypeStruct((rows, width), BF16),
        compiler_params=limit(8),
        cost_estimate=cost(pairs * 20_000_000, 6 * rows * width * 2),
    )(within, high, low, raw_gating_signal, group_layernorm_scaling[None, :], entering)

    mixed = lax.all_gather(mixed, "x", axis=0)
    place = jnp.stack([ic, ix * nz * vocab_local + head * share]).astype(jnp.int32)
    half = jax.ShapeDtypeStruct((ny * nx * own, embed // nx), F32)
    smem = pl.BlockSpec(memory_space=pltpu.SMEM)
    mine, theirs = pl.pallas_call(
        functools.partial(project_kernel, (ny, nc, own)),
        grid=(1,),
        in_specs=[
            smem,
            whole(nx, rows, width),
            pl.BlockSpec((nz, held, embed), lambda i: (0, 0, 0)),
        ],
        out_specs=[whole(*half.shape)] * 2,
        out_shape=[half, half],
        scratch_shapes=[pltpu.VMEM((nz * own_columns, width), BF16)],
        compiler_params=limit(24),
        cost_estimate=cost(4 * half.size * width, 4_000_000),
    )(place, mixed, in_hbm(gathered_1.reshape(nz, held + early, embed)))
    partial = mine + shifted(theirs, "c", 1)
    partial = partial.reshape(ny * nx, own, embed // nx)
    partial, facts = lax.optimization_barrier((partial, facts))
    facts = spread(facts, "x", [list(range(nx))])
    partial = lax.all_to_all(partial, ("y", "x"), 0, 0, tiled=True)
    projected = jnp.sum(partial.reshape(ny, nx, own, embed // nx), axis=0)
    projected = projected.transpose(1, 0, 2).reshape(own, embed)
    hidden = skip_stream_input.astype(F32) + projected
    hmean = jnp.mean(hidden, axis=-1, keepdims=True)
    hvar = jnp.mean((hidden - hmean) ** 2, axis=-1, keepdims=True)
    normed = ((hidden - hmean) / jnp.sqrt(hvar + 1e-05) * closing_layernorm_scaling).astype(BF16)

    normed, facts = lax.optimization_barrier((normed, facts))

    tokens = copies(normed, ("y", "x")).reshape(ny * nx * own, embed)
    facts = facts[..., 0, : 3 * own].reshape(nx, ny, nc, 3, own).transpose(3, 2, 1, 0, 4)
    other = shifted(tokens, "c", 1)
    count = plane * own
    labels = facts[0].reshape(1, count).astype(jnp.int32)
    def score(vocab, layout, tile, known=None):
        first, height = known is None, 3 if known is None else 2
        return pl.pallas_call(
            functools.partial(score_kernel, layout, first, not first),
            grid=(vocab.shape[0] // tile,),
            in_specs=[
                smem,
                vmem,
                vmem,
                vmem,
                pl.BlockSpec((tile, embed), lambda i: (i, 0)),
            ]
            + ([] if first else [vmem]),
            out_specs=whole(height, count),
            out_shape=jax.ShapeDtypeStruct((height, count), F32),
            scratch_shapes=[pltpu.VMEM((3, count), F32)],
            compiler_params=limit(24),
            cost_estimate=cost(
                2 * count * vocab.shape[0] * embed, (count + vocab.shape[0]) * embed * 2
            ),
        )(place, tokens, other, labels, in_hbm(vocab), *([] if first else [known]))

    known = score(gathered_1, (held + early, held, 0, vocab_local), gathered_1.shape[0])
    late = gathered_2.shape[0] // 2
    both = score(gathered_2, (share - early, 0, early, vocab_local), late, known)
    both = copies(both, ("x", "y", "c"))
    part, picked = both[:, 0], both[:, 1]
    peak = jnp.max(part, axis=0)
    logp = jnp.sum(picked, axis=0) - peak - jnp.log(jnp.sum(jnp.exp(part - peak), axis=0))
    ratio = facts[1] * (logp.reshape(nc, ny, nx, own) - facts[2])
    token_ratio = lax.dynamic_slice(ratio, (ic, iy, ix, 0), (1, 1, 1, own)).reshape(own)

    sums = jnp.sum(ratio, axis=(0, 1, 3))
    sums = copies(jnp.pad(sums, (0, LANES - nx)).reshape(1, LANES), "z")[:, 0, :nx]
    seq_of = rollout_for_segment.reshape(nx, nz).T
    marker = jnp.arange(query_text_for_rollout.shape[0])[:, None, None] == seq_of[None]
    seq_ratio = jnp.sum(jnp.where(marker, sums[None], 0.0), axis=(1, 2)) / TOK_BLK
    return (token_ratio, seq_ratio)


def solution(mesh):
    n_blk, n_head = mesh.devices.shape
    nx, nc = 4, 2
    fine = Mesh(
        mesh.devices.reshape(nx, n_blk // nx, n_head // nc, nc), ("x", "z", "y", "c")
    )
    blk, head = ("x", "z"), ("y", "c")
    placed = (
        P(blk, head),
        P(blk, head),
        P(blk, head),
        P(blk, head),
        P(blk, head),
        P(head),
        P(None, head, None),
        P(head),
        P(),
        P(blk + head, None),
        P(head, blk),
        P(blk, None),
        P(blk + head),
        P(blk + head),
        P(blk + head),
        P(),
        P(),
    )
    return jax.shard_map(
        per_device, mesh=fine, in_specs=placed, out_specs=(P(blk + head), P()), check_vma=False
    )
```

```python
import functools

import jax
import jax.numpy as jnp
from jax import lax
from jax.experimental import pallas as pl
from jax.experimental.pallas import tpu as pltpu
from jax.sharding import Mesh
from jax.sharding import PartitionSpec as P

CHAN = 64
LANES = 128
TOK_BLK = 128
SUB = 32
F32 = jnp.float32
BF16 = jnp.bfloat16


def parts2(a):
    high = a.astype(BF16)
    return high, (a - high.astype(F32)).astype(BF16)


def parts3(a):
    high, rest = a.astype(BF16), None
    rest = a - high.astype(F32)
    mid = rest.astype(BF16)
    return high, mid, (rest - mid.astype(F32)).astype(BF16)


def mm(a, b):
    return jnp.dot(a, b, preferred_element_type=F32)


def mm_t(a, b):
    return lax.dot_general(a, b, (((1,), (1,)), ((), ())), preferred_element_type=F32)


def running_log_decay(rate):
    log_decay = -jnp.exp(rate.astype(F32))
    rows = log_decay.shape[0]
    i = lax.broadcasted_iota(jnp.int32, (rows, rows), 0)
    j = lax.broadcasted_iota(jnp.int32, (rows, rows), 1)
    lower = (i >= j).astype(F32).astype(BF16)
    total = mm(
        jnp.concatenate([lower] * 3, axis=1), jnp.concatenate(parts3(log_decay), axis=0)
    )
    return log_decay, total


def left_lanes(rows):
    return lax.broadcasted_iota(jnp.int32, (rows, LANES), 1) < CHAN


def block_end_kernel(chunk_rows, k_ref, v_ref, w_ref, out_ref):
    _, inclusive = running_log_decay(w_ref[...])
    last = inclusive[TOK_BLK - 1 :, :]
    late = k_ref[...].astype(F32) * jnp.exp(last - inclusive)
    high, low = parts2(late.T)
    v = v_ref[...]
    both = mm(jnp.concatenate([high, low], axis=1), jnp.concatenate([v, v], axis=0))
    fall = jnp.exp(jnp.broadcast_to(last, (LANES, LANES)).T)
    left = left_lanes(CHAN)
    both = jnp.where(left, both[:CHAN], both[CHAN:])
    fall = jnp.where(left, fall[:CHAN], fall[CHAN:])
    span = CHAN // chunk_rows
    row = lax.broadcasted_iota(jnp.int32, (CHAN, LANES), 0) % chunk_rows
    lane = lax.broadcasted_iota(jnp.int32, (CHAN, LANES), 1) % CHAN // span
    fall = jnp.where(row == lane, fall, 0.0)
    for q in range(span):
        for r in range(chunk_rows):
            at = q * chunk_rows + r
            out_ref[q, :, r * LANES : (r + 1) * LANES] = both[at : at + 1]
        rows = slice(q * chunk_rows, (q + 1) * chunk_rows)
        out_ref[q, :, chunk_rows * LANES :] = jnp.sum(fall[rows], axis=0, keepdims=True)


def relay_kernel(chunk_rows, meta_ref, moved_ref, prompt_ref, out_ref):
    left = left_lanes(chunk_rows)
    row = lax.broadcasted_iota(jnp.int32, (chunk_rows, LANES), 0)
    lane = lax.broadcasted_iota(jnp.int32, (chunk_rows, LANES), 1) % CHAN
    chosen = lane == row * (CHAN // chunk_rows)

    def step(b, state):
        prompt = jnp.where(meta_ref[1, b] == 0, prompt_ref[0], prompt_ref[1])
        state = jnp.where(meta_ref[0, b] != 0, prompt, state)
        out_ref[b] = state
        change = jnp.concatenate(
            [moved_ref[b, :, r * LANES : (r + 1) * LANES] for r in range(chunk_rows)], axis=0
        )
        fall = moved_ref[b, :, chunk_rows * LANES :]
        fall = jnp.where(chosen, jnp.broadcast_to(fall, (chunk_rows, LANES)), 0.0)
        first = jnp.sum(jnp.where(left, fall, 0.0), axis=1, keepdims=True)
        second = jnp.sum(jnp.where(left, 0.0, fall), axis=1, keepdims=True)
        return jnp.where(left, first, second) * state + change

    lax.fori_loop(
        0, moved_ref.shape[0], step, jnp.zeros((chunk_rows, LANES), F32), unroll=8
    )


def within_kernel(r_ref, k_ref, v_ref, w_ref, u_ref, wkv_ref, high_ref, low_ref):
    r = r_ref[...].astype(F32)
    k = k_ref[...].astype(F32)
    v = v_ref[...]
    log_decay, inclusive = running_log_decay(w_ref[...])
    exclusive = inclusive - log_decay
    left = left_lanes(SUB)
    pieces = []
    for sub in range(TOK_BLK // SUB):
        a, b = sub * SUB, (sub + 1) * SUB
        pivot = inclusive[a + SUB // 2 - 1 : a + SUB // 2, :]
        rs = r[a:b] * jnp.exp(exclusive[a:b] - pivot)
        ks = k[:b] * jnp.exp(pivot - inclusive[:b])
        rs = jnp.concatenate([jnp.where(left, rs, 0.0), jnp.where(left, 0.0, rs)], axis=0)
        rh, rl = parts2(rs)
        kh, kl = parts2(ks)
        scores = mm_t(
            jnp.concatenate([rh, rl, rh], axis=1), jnp.concatenate([kh, kh, kl], axis=1)
        )
        t = lax.broadcasted_iota(jnp.int32, scores.shape, 0) % SUB + a
        s = lax.broadcasted_iota(jnp.int32, scores.shape, 1)
        sh, sl = parts2(jnp.where(s < t, scores, 0.0))
        both = mm(sh, v[:b]) + mm(sl, v[:b])
        pieces.append(jnp.where(left, both[:SUB], both[SUB:]))
    now = mm(jnp.concatenate(parts2(r * k * u_ref[...]), axis=1), same_head(1.0))
    wkv_ref[...] = jnp.concatenate(pieces, axis=0) + now * v.astype(F32)
    high_ref[...], low_ref[...] = parts2(r * jnp.exp(exclusive))


def same_head(value):
    i = lax.broadcasted_iota(jnp.int32, (LANES, LANES), 0) // CHAN
    j = lax.broadcasted_iota(jnp.int32, (LANES, LANES), 1) // CHAN
    return jnp.concatenate([jnp.where(i == j, value, 0.0).astype(BF16)] * 2, axis=0)


def mix_kernel(wkv_ref, high_ref, low_ref, g_ref, scale_ref, state_ref, out_ref):
    state = state_ref[...]
    left = left_lanes(CHAN)
    state = jnp.concatenate([jnp.where(left, state, 0.0), jnp.where(left, 0.0, state)], axis=0)
    sh, sl = parts2(state)
    high = high_ref[...]
    wkv = wkv_ref[...] + mm(
        jnp.concatenate([high, low_ref[...], high], axis=1), jnp.concatenate([sh, sh, sl], axis=0)
    )
    mean_of = same_head(1.0 / CHAN)
    mean = mm(jnp.concatenate(parts2(wkv), axis=1), mean_of)
    off = wkv - mean
    var = mm(jnp.concatenate(parts2(off * off), axis=1), mean_of)
    g = g_ref[...].astype(F32)
    y = off / jnp.sqrt(var + 0.00064) * scale_ref[...]
    out_ref[...] = (y * (g / (1.0 + jnp.exp(-g)))).astype(out_ref.dtype)


def project_kernel(shape, place_ref, mixed_ref, block_ref, mine_ref, theirs_ref, columns_ref):
    ny, nc, own = shape
    fold, held = block_ref.shape[2] // columns_ref.shape[1], block_ref.shape[1]
    width = columns_ref.shape[1]
    for z in range(block_ref.shape[0]):
        for b in range(fold):
            at = (z * fold + b) * held
            columns_ref[at : at + held, :] = block_ref[z, :, b * width : (b + 1) * width]
    for out_ref, core in ((theirs_ref, 1 - place_ref[0]), (mine_ref, place_ref[0])):
        rows = [
            mixed_ref[x, pl.ds(pl.multiple_of((y * nc + core) * own, own), own), :]
            for y in range(ny)
            for x in range(mixed_ref.shape[0])
        ]
        out_ref[...] = mm_t(jnp.concatenate(rows, axis=0), columns_ref[...])


def score_kernel(
    layout, first, final, place_ref, mine_ref, theirs_ref, label_ref, vocab_ref, *refs
):
    group, skipped, offset, vocab_local = layout
    known_ref, refs = (None, refs) if first else (refs[0], refs[1:])
    out_ref, state_ref, held_ref, arrived = refs
    step = pl.program_id(0)
    tile, half = vocab_ref.shape[0], mine_ref.shape[0]
    core = place_ref[0]
    copy = pltpu.make_async_copy(theirs_ref, held_ref, arrived)

    @pl.when(step == 0)
    def _():
        copy.start()
        if first:
            state_ref[0:1] = jnp.full((1, 2 * half), -3.0e38, F32)
            state_ref[1:3] = jnp.zeros((2, 2 * half), F32)
        else:
            state_ref[...] = known_ref[...]

    index = step * tile + lax.broadcasted_iota(jnp.int32, (tile, 1), 0)
    source = lax.div(index, jnp.int32(group))
    row = index - source * group
    entry = jnp.where(
        row < skipped, -1, place_ref[1] + source * vocab_local + (row - skipped + offset)
    )
    for part, tokens in enumerate((mine_ref, held_ref)):
        if part:
            pl.when(step == 0)(copy.wait)
        at = slice(part * half, (part + 1) * half)
        label = jnp.where(core == part, label_ref[:, :half], label_ref[:, half:])
        logits = mm_t(vocab_ref[...], tokens[...])
        found = jnp.where(entry == label, logits, 0.0)
        if skipped:
            logits = jnp.where(entry < 0, -3.0e38, logits)
        old = state_ref[0:1, at]
        top = jnp.maximum(old, jnp.max(logits, axis=0, keepdims=True))
        fresh = jnp.sum(jnp.exp(logits - top), axis=0, keepdims=True)
        state_ref[1:2, at] = state_ref[1:2, at] * jnp.exp(old - top) + fresh
        state_ref[2:3, at] += jnp.sum(found, axis=0, keepdims=True)
        state_ref[0:1, at] = top

    @pl.when(step == pl.num_programs(0) - 1)
    def _():
        if not final:
            out_ref[...] = state_ref[...]
            return
        part = state_ref[0:1] + jnp.log(state_ref[1:2])
        both = jnp.concatenate([part, state_ref[2:3]], axis=0)
        left, right = both[:, :half], both[:, half:]
        both = jnp.concatenate(
            [jnp.where(core == 0, left, right), jnp.where(core == 0, right, left)], axis=1
        )
        out_ref[...] = jnp.broadcast_to(both[None], out_ref.shape)


def cost(flops, nbytes):
    return pl.CostEstimate(flops=flops, bytes_accessed=nbytes, transcendentals=0)


def limit(mib):
    return pltpu.CompilerParams(vmem_limit_bytes=mib * 1024 * 1024)


def in_hbm(value):
    return pltpu.with_memory_space_constraint(value, pltpu.HBM)


def whole(*shape):
    return pl.BlockSpec(shape, lambda i: (0,) * len(shape))


def shifted(value, axis, steps):
    count = lax.axis_size(axis)
    return lax.ppermute(value, axis, [(i, (i + steps) % count) for i in range(count)])


def copies(value, axes):
    count = lax.axis_size(axes)
    sent = jnp.broadcast_to(value[None], (count, *value.shape))
    return lax.all_to_all(sent, axes, 0, 0, tiled=True)


def spread(value, axis, groups):
    count = len(groups[0])
    place = sum(
        jnp.where(lax.axis_index(axis) == source, i, 0)
        for group in groups
        for i, source in enumerate(group)
    )
    out = jnp.zeros((count, *value.shape), value.dtype)
    for step in range(count):
        pairs = [(g[i], g[(i + step) % count]) for g in groups for i in range(count)]
        piece = lax.ppermute(value, axis, pairs) if step else value
        out = lax.dynamic_update_index_in_dim(out, piece, (place - step) % count, 0)
    return out


def per_device(
    acceptance_vector,
    lookup_vector_array,
    payload_vector_array,
    raw_gating_signal,
    raw_forgetting_rate,
    current_reward_vector,
    memory_following_query,
    group_layernorm_scaling,
    closing_layernorm_scaling,
    skip_stream_input,
    closing_projection,
    vocabulary_readout,
    following_labels,
    response_indicator,
    baseline_logarithmic_likelihood,
    rollout_for_segment,
    query_text_for_rollout,
):
    nx, nz, ny, nc = (lax.axis_size(a) for a in ("x", "z", "y", "c"))
    ix, iz, iy, ic = (lax.axis_index(a) for a in ("x", "z", "y", "c"))
    n_blk, n_head = nx * nz, ny * nc
    blk, head = ix * nz + iz, iy * nc + ic
    rows, width = acceptance_vector.shape
    embed = skip_stream_input.shape[1]
    pairs = width // LANES
    own = rows // n_head

    vocab_local = vocabulary_readout.shape[0]
    share = vocab_local // n_head
    own_columns = closing_projection.shape[1]
    fold = embed // width
    held = own_columns // fold
    early = share * 3 // 8
    block = closing_projection.T.reshape(fold, held, width).transpose(1, 0, 2).reshape(held, embed)
    rows_1 = jnp.concatenate(
        [block, lax.dynamic_slice_in_dim(vocabulary_readout, head * share, early)], axis=0
    )
    gathered_1 = lax.all_gather(rows_1, "z", axis=0, tiled=True)

    chunks = n_blk // pairs
    chunk_rows = CHAN // chunks
    col = pl.BlockSpec((rows, LANES), lambda p: (0, p))
    end = pl.pallas_call(
        functools.partial(block_end_kernel, chunk_rows),
        grid=(pairs,),
        in_specs=[col] * 3,
        out_specs=pl.BlockSpec((chunks, 1, (chunk_rows + 1) * LANES), lambda p: (p, 0, 0)),
        out_shape=jax.ShapeDtypeStruct((n_blk, 1, (chunk_rows + 1) * LANES), F32),
        compiler_params=limit(60),
        cost_estimate=cost(pairs * 20_000_000, 3 * rows * width * 2),
    )(lookup_vector_array, payload_vector_array, raw_forgetting_rate)
    moved = lax.all_to_all(end, ("x", "z"), 0, 0, tiled=True)

    facts, bonus, _ = lax.optimization_barrier(
        (
            jnp.concatenate(
                [
                    following_labels.astype(F32),
                    response_indicator.astype(F32),
                    baseline_logarithmic_likelihood,
                ]
            ),
            current_reward_vector[None, :],
            end,
        )
    )
    plane = nx * ny * nc
    facts = jnp.pad(facts, (0, LANES - 3 * own)).reshape(1, LANES)
    row = pl.BlockSpec((1, LANES), lambda p: (0, p))
    within, high, low = pl.pallas_call(
        within_kernel,
        grid=(pairs,),
        in_specs=[col] * 4 + [row],
        out_specs=[col] * 3,
        out_shape=[jax.ShapeDtypeStruct((rows, width), t) for t in (F32, BF16, BF16)],
        compiler_params=limit(60),
        cost_estimate=cost(pairs * 60_000_000, 8 * rows * width * 2),
    )(acceptance_vector, lookup_vector_array, payload_vector_array, raw_forgetting_rate, bonus)

    prev_seq = jnp.concatenate([jnp.full((1,), -1, jnp.int32), rollout_for_segment[:-1]])
    starts = (rollout_for_segment != prev_seq).astype(jnp.int32)
    meta = jnp.stack([starts, query_text_for_rollout[rollout_for_segment]])
    prompts = memory_following_query.shape[0]
    prompt = lax.dynamic_slice(
        memory_following_query.reshape(prompts, pairs, 2, CHAN, CHAN),
        (0, blk // chunks, 0, (blk % chunks) * chunk_rows, 0),
        (prompts, 1, 2, chunk_rows, CHAN),
    )[:, 0]
    prompt = prompt.transpose(0, 2, 1, 3).reshape(prompts, chunk_rows, LANES).astype(F32)
    vocabulary, within = lax.optimization_barrier((vocabulary_readout, within))
    rows_2 = lax.dynamic_slice_in_dim(vocabulary, head * share + early, share - early)
    moved, within, high, low, facts, rows_2, meta, prompt = lax.optimization_barrier(
        (moved, within, high, low, facts, rows_2, meta, prompt)
    )
    gathered_2 = lax.all_gather(rows_2, "z", axis=0, tiled=True)
    vmem = pl.BlockSpec(memory_space=pltpu.VMEM)
    entering = pl.pallas_call(
        functools.partial(relay_kernel, chunk_rows),
        in_specs=[pl.BlockSpec(memory_space=pltpu.SMEM), vmem, vmem],
        out_specs=vmem,
        out_shape=jax.ShapeDtypeStruct((n_blk, chunk_rows, LANES), F32),
        compiler_params=limit(4),
        cost_estimate=cost(1_000_000, 500_000),
    )(meta, moved, prompt)
    facts, _ = lax.optimization_barrier((facts, entering))
    entering = lax.all_to_all(entering, ("x", "z"), 0, 0, tiled=True)
    facts = spread(facts, "c", [list(range(nc))])
    facts = spread(facts, "y", [list(range(ny))])
    entering, facts = lax.optimization_barrier((entering, facts))
    entering = entering.reshape(pairs * CHAN, LANES)

    mixed = pl.pallas_call(
        mix_kernel,
        grid=(pairs,),
        in_specs=[col] * 4 + [row, pl.BlockSpec((CHAN, LANES), lambda p: (p, 0))],
        out_specs=col,
        out_shape=jax.ShapeDtypeStruct((rows, width), BF16),
        compiler_params=limit(8),
        cost_estimate=cost(pairs * 20_000_000, 6 * rows * width * 2),
    )(within, high, low, raw_gating_signal, group_layernorm_scaling[None, :], entering)

    mixed = lax.all_gather(mixed, "x", axis=0)
    place = jnp.stack([ic, ix * nz * vocab_local + head * share]).astype(jnp.int32)
    half = jax.ShapeDtypeStruct((ny * nx * own, embed // nx), F32)
    smem = pl.BlockSpec(memory_space=pltpu.SMEM)
    mine, theirs = pl.pallas_call(
        functools.partial(project_kernel, (ny, nc, own)),
        grid=(1,),
        in_specs=[
            smem,
            whole(nx, rows, width),
            pl.BlockSpec((nz, held, embed), lambda i: (0, 0, 0)),
        ],
        out_specs=[whole(*half.shape)] * 2,
        out_shape=[half, half],
        scratch_shapes=[pltpu.VMEM((nz * own_columns, width), BF16)],
        compiler_params=limit(24),
        cost_estimate=cost(4 * half.size * width, 4_000_000),
    )(place, mixed, in_hbm(gathered_1.reshape(nz, held + early, embed)))
    partial = mine + shifted(theirs, "c", 1)
    partial = partial.reshape(ny * nx, own, embed // nx)
    partial, facts = lax.optimization_barrier((partial, facts))
    facts = spread(facts, "x", [list(range(nx))])
    partial = lax.all_to_all(partial, ("y", "x"), 0, 0, tiled=True)
    projected = jnp.sum(partial.reshape(ny, nx, own, embed // nx), axis=0)
    projected = projected.transpose(1, 0, 2).reshape(own, embed)
    hidden = skip_stream_input.astype(F32) + projected
    hmean = jnp.mean(hidden, axis=-1, keepdims=True)
    hvar = jnp.mean((hidden - hmean) ** 2, axis=-1, keepdims=True)
    normed = ((hidden - hmean) / jnp.sqrt(hvar + 1e-05) * closing_layernorm_scaling).astype(BF16)

    normed, facts = lax.optimization_barrier((normed, facts))

    tokens = copies(normed, ("y", "x")).reshape(ny * nx * own, embed)
    facts = facts[..., 0, : 3 * own].reshape(nx, ny, nc, 3, own).transpose(3, 2, 1, 0, 4)
    other = shifted(tokens, "c", 1)
    count = plane * own
    labels = facts[0].reshape(1, count).astype(jnp.int32)
    def score(vocab, layout, tile, known=None):
        first = known is None
        out = (3, count) if first else (plane, 2, count)
        return pl.pallas_call(
            functools.partial(score_kernel, layout, first, not first),
            grid=(vocab.shape[0] // tile,),
            in_specs=[
                smem,
                vmem,
                pl.BlockSpec(memory_space=pl.ANY),
                vmem,
                pl.BlockSpec((tile, embed), lambda i: (i, 0)),
            ]
            + ([] if first else [vmem]),
            out_specs=whole(*out),
            out_shape=jax.ShapeDtypeStruct(out, F32),
            scratch_shapes=[
                pltpu.VMEM((3, count), F32),
                pltpu.VMEM((count // nc, embed), BF16),
                pltpu.SemaphoreType.DMA,
            ],
            compiler_params=limit(24),
            cost_estimate=cost(
                2 * count * vocab.shape[0] * embed, (count + vocab.shape[0]) * embed * 2
            ),
        )(place, tokens, other, labels, in_hbm(vocab), *([] if first else [known]))

    known = score(gathered_1, (held + early, held, 0, vocab_local), gathered_1.shape[0])
    late = gathered_2.shape[0] // 2
    both = score(gathered_2, (share - early, 0, early, vocab_local), late, known)
    both = lax.all_to_all(both, ("x", "y", "c"), 0, 0, tiled=True)
    part, picked = both[:, 0], both[:, 1]
    peak = jnp.max(part, axis=0)
    logp = jnp.sum(picked, axis=0) - peak - jnp.log(jnp.sum(jnp.exp(part - peak), axis=0))
    ratio = facts[1] * (logp.reshape(nc, ny, nx, own) - facts[2])
    token_ratio = lax.dynamic_slice(ratio, (ic, iy, ix, 0), (1, 1, 1, own)).reshape(own)

    sums = jnp.sum(ratio, axis=(0, 1, 3))
    sums = copies(jnp.pad(sums, (0, LANES - nx)).reshape(1, LANES), "z")[:, 0, :nx]
    seq_of = rollout_for_segment.reshape(nx, nz).T
    marker = jnp.arange(query_text_for_rollout.shape[0])[:, None, None] == seq_of[None]
    seq_ratio = jnp.sum(jnp.where(marker, sums[None], 0.0), axis=(1, 2)) / TOK_BLK
    return (token_ratio, seq_ratio)


def solution(mesh):
    n_blk, n_head = mesh.devices.shape
    nx, nc = 4, 2
    fine = Mesh(
        mesh.devices.reshape(nx, n_blk // nx, n_head // nc, nc), ("x", "z", "y", "c")
    )
    blk, head = ("x", "z"), ("y", "c")
    placed = (
        P(blk, head),
        P(blk, head),
        P(blk, head),
        P(blk, head),
        P(blk, head),
        P(head),
        P(None, head, None),
        P(head),
        P(),
        P(blk + head, None),
        P(head, blk),
        P(blk, None),
        P(blk + head),
        P(blk + head),
        P(blk + head),
        P(),
        P(),
    )
    return jax.shard_map(
        per_device, mesh=fine, in_specs=placed, out_specs=(P(blk + head), P()), check_vma=False
    )
```

```python
import functools

import jax
import jax.numpy as jnp
from jax import lax
from jax.experimental import pallas as pl
from jax.experimental.pallas import tpu as pltpu
from jax.sharding import Mesh
from jax.sharding import PartitionSpec as P

CHAN = 64
LANES = 128
TOK_BLK = 128
SUB = 32
F32 = jnp.float32
BF16 = jnp.bfloat16


def parts2(a):
    high = a.astype(BF16)
    return high, (a - high.astype(F32)).astype(BF16)


def parts3(a):
    high, rest = a.astype(BF16), None
    rest = a - high.astype(F32)
    mid = rest.astype(BF16)
    return high, mid, (rest - mid.astype(F32)).astype(BF16)


def mm(a, b):
    return jnp.dot(a, b, preferred_element_type=F32)


def mm_t(a, b):
    return lax.dot_general(a, b, (((1,), (1,)), ((), ())), preferred_element_type=F32)


def running_log_decay(rate):
    log_decay = -jnp.exp(rate.astype(F32))
    rows = log_decay.shape[0]
    i = lax.broadcasted_iota(jnp.int32, (rows, rows), 0)
    j = lax.broadcasted_iota(jnp.int32, (rows, rows), 1)
    lower = (i >= j).astype(F32).astype(BF16)
    total = mm(
        jnp.concatenate([lower] * 3, axis=1), jnp.concatenate(parts3(log_decay), axis=0)
    )
    return log_decay, total


def left_lanes(rows):
    return lax.broadcasted_iota(jnp.int32, (rows, LANES), 1) < CHAN


def block_end_kernel(chunk_rows, k_ref, v_ref, w_ref, out_ref):
    _, inclusive = running_log_decay(w_ref[...])
    last = inclusive[TOK_BLK - 1 :, :]
    late = k_ref[...].astype(F32) * jnp.exp(last - inclusive)
    high, low = parts2(late.T)
    v = v_ref[...]
    both = mm(jnp.concatenate([high, low], axis=1), jnp.concatenate([v, v], axis=0))
    fall = jnp.exp(jnp.broadcast_to(last, (LANES, LANES)).T)
    left = left_lanes(CHAN)
    both = jnp.where(left, both[:CHAN], both[CHAN:])
    fall = jnp.where(left, fall[:CHAN], fall[CHAN:])
    span = CHAN // chunk_rows
    row = lax.broadcasted_iota(jnp.int32, (CHAN, LANES), 0) % chunk_rows
    lane = lax.broadcasted_iota(jnp.int32, (CHAN, LANES), 1) % CHAN // span
    fall = jnp.where(row == lane, fall, 0.0)
    for q in range(span):
        for r in range(chunk_rows):
            at = q * chunk_rows + r
            out_ref[q, :, r * LANES : (r + 1) * LANES] = both[at : at + 1]
        rows = slice(q * chunk_rows, (q + 1) * chunk_rows)
        out_ref[q, :, chunk_rows * LANES :] = jnp.sum(fall[rows], axis=0, keepdims=True)


def relay_kernel(chunk_rows, meta_ref, moved_ref, prompt_ref, out_ref):
    left = left_lanes(chunk_rows)
    row = lax.broadcasted_iota(jnp.int32, (chunk_rows, LANES), 0)
    lane = lax.broadcasted_iota(jnp.int32, (chunk_rows, LANES), 1) % CHAN
    chosen = lane == row * (CHAN // chunk_rows)

    def step(b, state):
        prompt = jnp.where(meta_ref[1, b] == 0, prompt_ref[0], prompt_ref[1])
        state = jnp.where(meta_ref[0, b] != 0, prompt, state)
        out_ref[b] = state
        change = jnp.concatenate(
            [moved_ref[b, :, r * LANES : (r + 1) * LANES] for r in range(chunk_rows)], axis=0
        )
        fall = moved_ref[b, :, chunk_rows * LANES :]
        fall = jnp.where(chosen, jnp.broadcast_to(fall, (chunk_rows, LANES)), 0.0)
        first = jnp.sum(jnp.where(left, fall, 0.0), axis=1, keepdims=True)
        second = jnp.sum(jnp.where(left, 0.0, fall), axis=1, keepdims=True)
        return jnp.where(left, first, second) * state + change

    lax.fori_loop(
        0, moved_ref.shape[0], step, jnp.zeros((chunk_rows, LANES), F32), unroll=8
    )


def within_kernel(r_ref, k_ref, v_ref, w_ref, u_ref, wkv_ref, high_ref, low_ref):
    r = r_ref[...].astype(F32)
    k = k_ref[...].astype(F32)
    v = v_ref[...]
    log_decay, inclusive = running_log_decay(w_ref[...])
    exclusive = inclusive - log_decay
    left = left_lanes(SUB)
    pieces = []
    for sub in range(TOK_BLK // SUB):
        a, b = sub * SUB, (sub + 1) * SUB
        pivot = inclusive[a + SUB // 2 - 1 : a + SUB // 2, :]
        rs = r[a:b] * jnp.exp(exclusive[a:b] - pivot)
        ks = k[:b] * jnp.exp(pivot - inclusive[:b])
        rs = jnp.concatenate([jnp.where(left, rs, 0.0), jnp.where(left, 0.0, rs)], axis=0)
        rh, rl = parts2(rs)
        kh, kl = parts2(ks)
        scores = mm_t(
            jnp.concatenate([rh, rl, rh], axis=1), jnp.concatenate([kh, kh, kl], axis=1)
        )
        t = lax.broadcasted_iota(jnp.int32, scores.shape, 0) % SUB + a
        s = lax.broadcasted_iota(jnp.int32, scores.shape, 1)
        sh, sl = parts2(jnp.where(s < t, scores, 0.0))
        both = mm(sh, v[:b]) + mm(sl, v[:b])
        pieces.append(jnp.where(left, both[:SUB], both[SUB:]))
    now = mm(jnp.concatenate(parts2(r * k * u_ref[...]), axis=1), same_head(1.0))
    wkv_ref[...] = jnp.concatenate(pieces, axis=0) + now * v.astype(F32)
    high_ref[...], low_ref[...] = parts2(r * jnp.exp(exclusive))


def same_head(value):
    i = lax.broadcasted_iota(jnp.int32, (LANES, LANES), 0) // CHAN
    j = lax.broadcasted_iota(jnp.int32, (LANES, LANES), 1) // CHAN
    return jnp.concatenate([jnp.where(i == j, value, 0.0).astype(BF16)] * 2, axis=0)


def mix_kernel(wkv_ref, high_ref, low_ref, g_ref, scale_ref, state_ref, out_ref):
    state = state_ref[...]
    left = left_lanes(CHAN)
    state = jnp.concatenate([jnp.where(left, state, 0.0), jnp.where(left, 0.0, state)], axis=0)
    sh, sl = parts2(state)
    high = high_ref[...]
    wkv = wkv_ref[...] + mm(
        jnp.concatenate([high, low_ref[...], high], axis=1), jnp.concatenate([sh, sh, sl], axis=0)
    )
    mean_of = same_head(1.0 / CHAN)
    mean = mm(jnp.concatenate(parts2(wkv), axis=1), mean_of)
    off = wkv - mean
    var = mm(jnp.concatenate(parts2(off * off), axis=1), mean_of)
    g = g_ref[...].astype(F32)
    y = off / jnp.sqrt(var + 0.00064) * scale_ref[...]
    out_ref[...] = (y * (g / (1.0 + jnp.exp(-g)))).astype(out_ref.dtype)


def project_kernel(shape, place_ref, mixed_ref, block_ref, mine_ref, theirs_ref, columns_ref):
    ny, nc, own = shape
    fold, held = block_ref.shape[2] // columns_ref.shape[1], block_ref.shape[1]
    width = columns_ref.shape[1]
    for z in range(block_ref.shape[0]):
        for b in range(fold):
            at = (z * fold + b) * held
            columns_ref[at : at + held, :] = block_ref[z, :, b * width : (b + 1) * width]
    for out_ref, core in ((theirs_ref, 1 - place_ref[0]), (mine_ref, place_ref[0])):
        rows = [
            mixed_ref[x, pl.ds(pl.multiple_of((y * nc + core) * own, own), own), :]
            for y in range(ny)
            for x in range(mixed_ref.shape[0])
        ]
        out_ref[...] = mm_t(jnp.concatenate(rows, axis=0), columns_ref[...])


def score_kernel(
    layout, first, final, place_ref, mine_ref, theirs_ref, label_ref, vocab_ref, *refs
):
    group, skipped, offset, vocab_local = layout
    known_ref, (out_ref, state_ref) = (None, refs) if first else (refs[0], refs[1:])
    step = pl.program_id(0)
    tile, half = vocab_ref.shape[0], mine_ref.shape[0]
    core = place_ref[0]

    @pl.when(step == 0)
    def _():
        if first:
            state_ref[0:1] = jnp.full((1, 2 * half), -3.0e38, F32)
            state_ref[1:3] = jnp.zeros((2, 2 * half), F32)
        else:
            state_ref[...] = known_ref[...]

    index = step * tile + lax.broadcasted_iota(jnp.int32, (tile, 1), 0)
    source = lax.div(index, jnp.int32(group))
    row = index - source * group
    entry = jnp.where(
        row >= group - skipped, -1, place_ref[1] + source * vocab_local + (row + offset)
    )
    for part, tokens in enumerate((mine_ref, theirs_ref)):
        at = slice(part * half, (part + 1) * half)
        label = jnp.where(core == part, label_ref[:, :half], label_ref[:, half:])
        logits = mm_t(vocab_ref[...], tokens[...])
        found = jnp.where(entry == label, logits, 0.0)
        if skipped:
            logits = jnp.where(entry < 0, -3.0e38, logits)
        old = state_ref[0:1, at]
        top = jnp.maximum(old, jnp.max(logits, axis=0, keepdims=True))
        fresh = jnp.sum(jnp.exp(logits - top), axis=0, keepdims=True)
        state_ref[1:2, at] = state_ref[1:2, at] * jnp.exp(old - top) + fresh
        state_ref[2:3, at] += jnp.sum(found, axis=0, keepdims=True)
        state_ref[0:1, at] = top

    @pl.when(step == pl.num_programs(0) - 1)
    def _():
        if not final:
            out_ref[...] = state_ref[...]
            return
        part = state_ref[0:1] + jnp.log(state_ref[1:2])
        both = jnp.concatenate([part, state_ref[2:3]], axis=0)
        left, right = both[:, :half], both[:, half:]
        both = jnp.concatenate(
            [jnp.where(core == 0, left, right), jnp.where(core == 0, right, left)], axis=1
        )
        out_ref[...] = jnp.broadcast_to(both[None], out_ref.shape)


def cost(flops, nbytes):
    return pl.CostEstimate(flops=flops, bytes_accessed=nbytes, transcendentals=0)


def limit(mib):
    return pltpu.CompilerParams(vmem_limit_bytes=mib * 1024 * 1024)


def in_hbm(value):
    return pltpu.with_memory_space_constraint(value, pltpu.HBM)


def whole(*shape):
    return pl.BlockSpec(shape, lambda i: (0,) * len(shape))


def shifted(value, axis, steps):
    count = lax.axis_size(axis)
    return lax.ppermute(value, axis, [(i, (i + steps) % count) for i in range(count)])


def copies(value, axes):
    count = lax.axis_size(axes)
    sent = jnp.broadcast_to(value[None], (count, *value.shape))
    return lax.all_to_all(sent, axes, 0, 0, tiled=True)


def spread(value, axis, groups):
    count = len(groups[0])
    place = sum(
        jnp.where(lax.axis_index(axis) == source, i, 0)
        for group in groups
        for i, source in enumerate(group)
    )
    out = jnp.zeros((count, *value.shape), value.dtype)
    for step in range(count):
        pairs = [(g[i], g[(i + step) % count]) for g in groups for i in range(count)]
        piece = lax.ppermute(value, axis, pairs) if step else value
        out = lax.dynamic_update_index_in_dim(out, piece, (place - step) % count, 0)
    return out


def per_device(
    acceptance_vector,
    lookup_vector_array,
    payload_vector_array,
    raw_gating_signal,
    raw_forgetting_rate,
    current_reward_vector,
    memory_following_query,
    group_layernorm_scaling,
    closing_layernorm_scaling,
    skip_stream_input,
    closing_projection,
    vocabulary_readout,
    following_labels,
    response_indicator,
    baseline_logarithmic_likelihood,
    rollout_for_segment,
    query_text_for_rollout,
):
    nx, nz, ny, nc = (lax.axis_size(a) for a in ("x", "z", "y", "c"))
    ix, iz, iy, ic = (lax.axis_index(a) for a in ("x", "z", "y", "c"))
    n_blk, n_head = nx * nz, ny * nc
    blk, head = ix * nz + iz, iy * nc + ic
    rows, width = acceptance_vector.shape
    embed = skip_stream_input.shape[1]
    pairs = width // LANES
    own = rows // n_head

    vocab_local = vocabulary_readout.shape[0]
    share = vocab_local // n_head
    own_columns = closing_projection.shape[1]
    fold = embed // width
    held = own_columns // fold
    early = share * 3 // 8
    block = closing_projection.T.reshape(fold, held, width).transpose(1, 0, 2).reshape(held, embed)
    rows_1 = lax.dynamic_slice_in_dim(vocabulary_readout, head * share, early + held)
    rows_1 = lax.dynamic_update_slice_in_dim(rows_1, block, early, 0)
    gathered_1 = lax.all_gather(rows_1, "z", axis=0, tiled=True)

    chunks = n_blk // pairs
    chunk_rows = CHAN // chunks
    col = pl.BlockSpec((rows, LANES), lambda p: (0, p))
    end = pl.pallas_call(
        functools.partial(block_end_kernel, chunk_rows),
        grid=(pairs,),
        in_specs=[col] * 3,
        out_specs=pl.BlockSpec((chunks, 1, (chunk_rows + 1) * LANES), lambda p: (p, 0, 0)),
        out_shape=jax.ShapeDtypeStruct((n_blk, 1, (chunk_rows + 1) * LANES), F32),
        compiler_params=limit(60),
        cost_estimate=cost(pairs * 20_000_000, 3 * rows * width * 2),
    )(lookup_vector_array, payload_vector_array, raw_forgetting_rate)
    moved = lax.all_to_all(end, ("x", "z"), 0, 0, tiled=True)

    facts, bonus, _ = lax.optimization_barrier(
        (
            jnp.concatenate(
                [
                    following_labels.astype(F32),
                    response_indicator.astype(F32),
                    baseline_logarithmic_likelihood,
                ]
            ),
            current_reward_vector[None, :],
            end,
        )
    )
    plane = nx * ny * nc
    facts = jnp.pad(facts, (0, LANES - 3 * own)).reshape(1, LANES)
    row = pl.BlockSpec((1, LANES), lambda p: (0, p))
    within, high, low = pl.pallas_call(
        within_kernel,
        grid=(pairs,),
        in_specs=[col] * 4 + [row],
        out_specs=[col] * 3,
        out_shape=[jax.ShapeDtypeStruct((rows, width), t) for t in (F32, BF16, BF16)],
        compiler_params=limit(60),
        cost_estimate=cost(pairs * 60_000_000, 8 * rows * width * 2),
    )(acceptance_vector, lookup_vector_array, payload_vector_array, raw_forgetting_rate, bonus)

    prev_seq = jnp.concatenate([jnp.full((1,), -1, jnp.int32), rollout_for_segment[:-1]])
    starts = (rollout_for_segment != prev_seq).astype(jnp.int32)
    meta = jnp.stack([starts, query_text_for_rollout[rollout_for_segment]])
    prompts = memory_following_query.shape[0]
    prompt = lax.dynamic_slice(
        memory_following_query.reshape(prompts, pairs, 2, CHAN, CHAN),
        (0, blk // chunks, 0, (blk % chunks) * chunk_rows, 0),
        (prompts, 1, 2, chunk_rows, CHAN),
    )[:, 0]
    prompt = prompt.transpose(0, 2, 1, 3).reshape(prompts, chunk_rows, LANES).astype(F32)
    vocabulary, within = lax.optimization_barrier((vocabulary_readout, within))
    rows_2 = lax.dynamic_slice_in_dim(vocabulary, head * share + early, share - early)
    moved, within, high, low, facts, rows_2, meta, prompt = lax.optimization_barrier(
        (moved, within, high, low, facts, rows_2, meta, prompt)
    )
    gathered_2 = lax.all_gather(rows_2, "z", axis=0, tiled=True)
    vmem = pl.BlockSpec(memory_space=pltpu.VMEM)
    entering = pl.pallas_call(
        functools.partial(relay_kernel, chunk_rows),
        in_specs=[pl.BlockSpec(memory_space=pltpu.SMEM), vmem, vmem],
        out_specs=vmem,
        out_shape=jax.ShapeDtypeStruct((n_blk, chunk_rows, LANES), F32),
        compiler_params=limit(4),
        cost_estimate=cost(1_000_000, 500_000),
    )(meta, moved, prompt)
    facts, _ = lax.optimization_barrier((facts, entering))
    entering = lax.all_to_all(entering, ("x", "z"), 0, 0, tiled=True)
    facts = spread(facts, "c", [list(range(nc))])
    facts = spread(facts, "y", [list(range(ny))])
    entering, facts = lax.optimization_barrier((entering, facts))
    entering = entering.reshape(pairs * CHAN, LANES)

    mixed = pl.pallas_call(
        mix_kernel,
        grid=(pairs,),
        in_specs=[col] * 4 + [row, pl.BlockSpec((CHAN, LANES), lambda p: (p, 0))],
        out_specs=col,
        out_shape=jax.ShapeDtypeStruct((rows, width), BF16),
        compiler_params=limit(8),
        cost_estimate=cost(pairs * 20_000_000, 6 * rows * width * 2),
    )(within, high, low, raw_gating_signal, group_layernorm_scaling[None, :], entering)

    mixed = lax.all_gather(mixed, "x", axis=0)
    place = jnp.stack([ic, ix * nz * vocab_local + head * share]).astype(jnp.int32)
    half = jax.ShapeDtypeStruct((ny * nx * own, embed // nx), F32)
    smem = pl.BlockSpec(memory_space=pltpu.SMEM)
    mine, theirs = pl.pallas_call(
        functools.partial(project_kernel, (ny, nc, own)),
        grid=(1,),
        in_specs=[
            smem,
            whole(nx, rows, width),
            pl.BlockSpec((nz, held, embed), lambda i: (0, early // held, 0)),
        ],
        out_specs=[whole(*half.shape)] * 2,
        out_shape=[half, half],
        scratch_shapes=[pltpu.VMEM((nz * own_columns, width), BF16)],
        compiler_params=limit(24),
        cost_estimate=cost(4 * half.size * width, 4_000_000),
    )(place, mixed, in_hbm(gathered_1.reshape(nz, held + early, embed)))
    partial = mine + shifted(theirs, "c", 1)
    partial = partial.reshape(ny * nx, own, embed // nx)
    partial, facts = lax.optimization_barrier((partial, facts))
    facts = spread(facts, "x", [list(range(nx))])
    partial = lax.all_to_all(partial, ("y", "x"), 0, 0, tiled=True)
    projected = jnp.sum(partial.reshape(ny, nx, own, embed // nx), axis=0)
    projected = projected.transpose(1, 0, 2).reshape(own, embed)
    hidden = skip_stream_input.astype(F32) + projected
    hmean = jnp.mean(hidden, axis=-1, keepdims=True)
    hvar = jnp.mean((hidden - hmean) ** 2, axis=-1, keepdims=True)
    normed = ((hidden - hmean) / jnp.sqrt(hvar + 1e-05) * closing_layernorm_scaling).astype(BF16)

    normed, facts = lax.optimization_barrier((normed, facts))

    tokens = copies(normed, ("y", "x")).reshape(ny * nx * own, embed)
    facts = facts[..., 0, : 3 * own].reshape(nx, ny, nc, 3, own).transpose(3, 2, 1, 0, 4)
    other = shifted(tokens, "c", 1)
    count = plane * own
    labels = facts[0].reshape(1, count).astype(jnp.int32)
    def score(vocab, layout, tile, known=None):
        first = known is None
        out = (3, count) if first else (plane, 2, count)
        return pl.pallas_call(
            functools.partial(score_kernel, layout, first, not first),
            grid=(vocab.shape[0] // tile,),
            in_specs=[
                smem,
                vmem,
                vmem,
                vmem,
                pl.BlockSpec((tile, embed), lambda i: (i, 0)),
            ]
            + ([] if first else [vmem]),
            out_specs=whole(*out),
            out_shape=jax.ShapeDtypeStruct(out, F32),
            scratch_shapes=[pltpu.VMEM((3, count), F32)],
            compiler_params=limit(24),
            cost_estimate=cost(
                2 * count * vocab.shape[0] * embed, (count + vocab.shape[0]) * embed * 2
            ),
        )(place, tokens, other, labels, in_hbm(vocab), *([] if first else [known]))

    known = score(gathered_1, (held + early, held, 0, vocab_local), gathered_1.shape[0])
    late = gathered_2.shape[0] // 2
    both = score(gathered_2, (share - early, 0, early, vocab_local), late, known)
    both = lax.all_to_all(both, ("x", "y", "c"), 0, 0, tiled=True)
    part, picked = both[:, 0], both[:, 1]
    peak = jnp.max(part, axis=0)
    logp = jnp.sum(picked, axis=0) - peak - jnp.log(jnp.sum(jnp.exp(part - peak), axis=0))
    ratio = facts[1] * (logp.reshape(nc, ny, nx, own) - facts[2])
    token_ratio = lax.dynamic_slice(ratio, (ic, iy, ix, 0), (1, 1, 1, own)).reshape(own)

    sums = jnp.sum(ratio, axis=(0, 1, 3))
    sums = copies(jnp.pad(sums, (0, LANES - nx)).reshape(1, LANES), "z")[:, 0, :nx]
    seq_of = rollout_for_segment.reshape(nx, nz).T
    marker = jnp.arange(query_text_for_rollout.shape[0])[:, None, None] == seq_of[None]
    seq_ratio = jnp.sum(jnp.where(marker, sums[None], 0.0), axis=(1, 2)) / TOK_BLK
    return (token_ratio, seq_ratio)


def solution(mesh):
    n_blk, n_head = mesh.devices.shape
    nx, nc = 4, 2
    fine = Mesh(
        mesh.devices.reshape(nx, n_blk // nx, n_head // nc, nc), ("x", "z", "y", "c")
    )
    blk, head = ("x", "z"), ("y", "c")
    placed = (
        P(blk, head),
        P(blk, head),
        P(blk, head),
        P(blk, head),
        P(blk, head),
        P(head),
        P(None, head, None),
        P(head),
        P(),
        P(blk + head, None),
        P(head, blk),
        P(blk, None),
        P(blk + head),
        P(blk + head),
        P(blk + head),
        P(),
        P(),
    )
    return jax.shard_map(
        per_device, mesh=fine, in_specs=placed, out_specs=(P(blk + head), P()), check_vma=False
    )
```
